256 devices in a mesh: row: 32 (over z_hi, y, core), col: 8 (over z_lo, x).
Axes of the slice: x: 4, y: 4, z: 8 (z_hi: 4, z_lo: 2; z = z_hi * 2 + z_lo), core: 2. Of those that a mesh axis runs over, the one named last changes fastest.
Arguments:
- left: float32 [128, 16384], P('col', 'row'), may hold values from -12 to 12
- right: float32 [128, 16384], P('row', 'col'), may hold values from -12 to 12
- w_out: float32 [1024, 128], replicated, may hold values from -0.1875 to 0.1875
- b_out: float32 [128], replicated, may hold values from -3 to 3
- pair_grad: float32 [512, 512, 128], P('row', 'col'), may hold values from -6 to 6
Outputs:
- pair_out: float32 [512, 512, 128], P('row', 'col')
- grad_left: float32 [128, 16384], P('col', 'row')
- grad_right: float32 [128, 16384], P('row', 'col')
- grad_weight: float32 [1024, 128], replicated
- grad_bias: float32 [128], replicated
The draws below stay inside these ranges and needn't reach their ends.
All inputs are finite; a program needn't handle non-finite values.
Results may differ from the reference program's by a relative error of at most 0.0001.
Values sent between devices are 32-bit elements; how exact they have to be, the bound alone decides.
No kernel may reach another device: no remote copies, remote signals or barrier semaphores. Data moves between devices by JAX's collectives and lax.ppermute only.
A program may use at most 128 MiB of HBM per device.

```python
import jax
import jax.numpy as jnp
from jax import lax

C = 32
Z = 128
S = 128
R = 512
N_ROW = 32


def shard_levels(rng, dims, cuts, least, top_value):
    loudness = 1.0
    for position, blocks in cuts:
        draws = jax.random.uniform(jax.random.fold_in(jax.random.fold_in(rng, 6), position), (blocks,), jnp.float32, least / len(cuts), top_value / len(cuts))
        loudness = loudness * jnp.repeat(jnp.exp(draws), dims[position] // blocks).reshape((-1,) + (1,) * (len(dims) - 1 - position))
    return loudness


def normal_values(key, extent, deviation, reach, pieces=(), held_as=jnp.bfloat16):
    values = deviation * jax.random.normal(key, extent, jnp.float32)
    if pieces:
        values = values * shard_levels(key, extent, pieces, -0.22, 0.18)
    return jnp.clip(values, -reach, reach).astype(held_as)


def setup_inputs(seed: int = 0) -> dict:
    streams_of = jax.random.split(jax.random.key(seed), 6)
    return {
        "left": normal_values(streams_of[0], (S, R * C), 2.0, 12.0, ((0, 8), (1, 32)), jnp.float32),
        "right": normal_values(streams_of[1], (S, R * C), 2.0, 12.0, ((0, 32), (1, 8)), jnp.float32),
        "w_out": normal_values(streams_of[2], (C * C, Z), (C * C) ** -0.5, 0.1875, (), jnp.float32),
        "b_out": normal_values(streams_of[3], (Z,), 0.5, 3.0, (), jnp.float32),
        "pair_grad": normal_values(streams_of[4], (R, R, Z), 1.0, 6.0, ((0, 32), (1, 8)), jnp.float32),
    }


def reference(left, right, w_out, b_out, pair_grad):
    highest = lax.Precision.HIGHEST
    block_rows = R // N_ROW
    weight_cube = w_out.reshape(C, C, Z)

    def advance(carry, block_index):
        sum_right, sum_weight, sum_bias = carry
        left_block = lax.dynamic_slice_in_dim(left, block_index * (block_rows * C), block_rows * C, 1)
        outer = lax.dot_general(left_block, right, (((0,), (0,)), ((), ())), precision=highest,
                                preferred_element_type=jnp.float32) / S
        outer_split = outer.reshape(block_rows, C, R, C)
        grad_tile = lax.dynamic_slice_in_dim(pair_grad, block_index * block_rows, block_rows, 0)
        out_block = jnp.einsum("icje,cez->ijz", outer_split, weight_cube, precision=highest) + b_out
        grad_outer = jnp.einsum("ijz,cez->icje", grad_tile, weight_cube, precision=highest)
        grad_outer = grad_outer.reshape(block_rows * C, R * C)
        left_block_grad = lax.dot_general(right, grad_outer, (((1,), (1,)), ((), ())), precision=highest,
                                          preferred_element_type=jnp.float32) / S
        right_term = jnp.dot(left_block, grad_outer, precision=highest) / S
        weight_term = jnp.einsum("icje,ijz->cez", outer_split, grad_tile, precision=highest)
        carry = (sum_right + right_term, sum_weight + weight_term, sum_bias + jnp.sum(grad_tile, axis=(0, 1)))
        return carry, (out_block, left_block_grad)

    start_carry = (jnp.zeros((S, R * C), jnp.float32), jnp.zeros((C, C, Z), jnp.float32),
                   jnp.zeros((Z,), jnp.float32))
    (grad_right, sum_weight, sum_bias), (outs, lefts) = lax.scan(
        advance, start_carry, jnp.arange(N_ROW, dtype=jnp.int32))
    pair_out = outs.reshape(R, R, Z)
    grad_left = jnp.transpose(lefts, (1, 0, 2)).reshape(S, R * C)
    grad_weight = sum_weight.reshape(C * C, Z) / R
    grad_bias = sum_bias / R
    return (pair_out, grad_left, grad_right, grad_weight, grad_bias)
```

```python
import jax
import jax.numpy as jnp
from jax import lax
from jax.experimental import pallas as pl
from jax.experimental.pallas import tpu as pltpu
from jax.sharding import PartitionSpec as P

C = 32
Z = 128
S = 128
TI = 16
TJ = 64
IC = TI * C
JE = TJ * C
IJ = TI * TJ
CE = C * C
F32 = jnp.float32
BF16 = jnp.bfloat16
NT = (((1,), (1,)), ((), ()))
NN = (((1,), (0,)), ((), ()))


def split(x):
    hi = x.astype(BF16)
    return hi, (x - hi.astype(F32)).astype(BF16)


def dot(x, y, dims=NN):
    return lax.dot_general(x, y, dims, preferred_element_type=F32)


def half_swap(x0, x1):
    lane = lax.broadcasted_iota(jnp.int32, x0.shape, 1)
    low = lane < 64
    r0 = pltpu.roll(x0, 64, 1)
    r1 = pltpu.roll(x1, 64, 1)
    return jnp.where(low, x0, r1), jnp.where(low, r0, x1)


def core_index():
    return lax.rem(lax.axis_index("row"), 2)


def order_left(left_ref, core):
    own, other = [], []
    for k in range(16):
        lo = left_ref[8 * k : 8 * k + 4, :]
        hi = left_ref[8 * k + 4 : 8 * k + 8, :]
        own.append(jnp.where(core == 0, lo, hi))
        other.append(jnp.where(core == 0, hi, lo))
    return own + other


def load_left(left_ref, a_scr, core):
    for k, part in enumerate(order_left(left_ref, core)):
        a_scr[4 * k : 4 * k + 4, :] = part


def load_weight(w_ref, wp_scr):
    for e in range(C):
        wp_scr[C * e : C * e + C, :] = w_ref[pl.ds(e, C, stride=C), :]


def grad_outer_kernel(g_ref, w_ref, goh_ref, gol_ref, wp_scr, r_scr):
    load_weight(w_ref, wp_scr)
    wh, wl = split(wp_scr[...])
    wcat = jnp.concatenate([wh, wl], axis=1)

    @pl.loop(0, 4)
    def _(n):
        gh, gl = split(g_ref[pl.ds(pl.multiple_of(n * 256, 256), 256), :])
        r_scr[...] = dot(wcat, jnp.concatenate([gh, gh], axis=1), NT) + dot(wh, gl, NT)
        for ip in range(2):
            for ep in range(16):
                x0 = r_scr[64 * ep : 64 * ep + 32, 128 * ip : 128 * ip + 128]
                x1 = r_scr[64 * ep + 32 : 64 * ep + 64, 128 * ip : 128 * ip + 128]
                for k, y in enumerate(half_swap(x0, x1)):
                    hi, lo = split(y)
                    rows = pl.ds(pl.multiple_of((4 * n + 2 * ip + k) * C, C), C)
                    goh_ref[rows, 128 * ep : 128 * ep + 128] = hi
                    gol_ref[rows, 128 * ep : 128 * ep + 128] = lo


def grad_right_kernel(left_ref, goh_ref, gol_ref, own_ref, other_ref, a_scr, t_scr):
    load_left(left_ref, a_scr, core_index())
    ah, al = split(a_scr[...])
    acat = jnp.concatenate([ah, al], axis=0)

    @pl.loop(0, 8)
    def _(n):
        cols = pl.ds(pl.multiple_of(n * 256, 256), 256)
        r = dot(acat, goh_ref[:, cols])
        r = r[:S] + r[S:] + dot(ah, gol_ref[:, cols])
        t_scr[cols, :] = (r * (1.0 / S)).T

    for m in range(16):
        block = jnp.concatenate([t_scr[pl.ds(4 * m + q, C, stride=TJ), :] for q in range(4)], axis=0)
        block = block.T
        for k in range(16):
            own_ref[k, :, 128 * m : 128 * m + 128] = block[4 * k : 4 * k + 4]
            other_ref[k, :, 128 * m : 128 * m + 128] = block[64 + 4 * k : 68 + 4 * k]


def outer_kernel(left_ref, own_ref, other_ref, g_ref, oh_ref, ol_ref, bh_ref, bl_ref, gwo_ref, gwx_ref,
                 a_scr, b_scr, t_scr, r_scr, w_scr):
    core = core_index()
    load_left(left_ref, a_scr, core)
    for k in range(16):
        b_scr[4 * k : 4 * k + 4, :] = own_ref[k]
        b_scr[64 + 4 * k : 68 + 4 * k, :] = other_ref[k]
    for m in range(16):
        t_scr[128 * m : 128 * m + 128, :] = b_scr[:, 128 * m : 128 * m + 128].T
    for e in range(C):
        hi, lo = split(t_scr[pl.ds(e, TJ, stride=C), :])
        bh_ref[TJ * e : TJ * e + TJ, :] = hi
        bl_ref[TJ * e : TJ * e + TJ, :] = lo
    ath, atl = split(a_scr[...].T)
    atcat = jnp.concatenate([ath, atl], axis=1)

    @pl.loop(0, 8)
    def _(n):
        rows = pl.ds(pl.multiple_of(n * 256, 256), 256)
        bh = bh_ref[rows, :]
        r_scr[...] = dot(atcat, jnp.concatenate([bh, bh], axis=1), NT) + dot(ath, bl_ref[rows, :], NT)
        for ep in range(2):
            for ip in range(8):
                x0 = r_scr[64 * ip : 64 * ip + 32, 128 * ep : 128 * ep + 128]
                x1 = r_scr[64 * ip + 32 : 64 * ip + 64, 128 * ep : 128 * ep + 128]
                for k, y in enumerate(half_swap(x0, x1)):
                    hi, lo = split(y)
                    out_rows = pl.ds(pl.multiple_of((4 * n + 2 * ep + k) * C, C), C)
                    oh_ref[out_rows, 128 * ip : 128 * ip + 128] = hi
                    ol_ref[out_rows, 128 * ip : 128 * ip + 128] = lo

    gh, gl = split(g_ref[...])
    gcat = jnp.concatenate([gh, gl], axis=1)

    @pl.loop(0, 4)
    def _(n):
        rows = pl.ds(pl.multiple_of(n * 256, 256), 256)
        r = dot(oh_ref[rows, :], gcat)
        w_scr[rows, :] = (r[:, :Z] + r[:, Z:] + dot(ol_ref[rows, :], gh)) * (1.0 / S)

    bias = jnp.broadcast_to(jnp.sum(g_ref[...], axis=0, keepdims=True), (8, Z))
    for k in range(16):
        lo = w_scr[pl.ds(k, C, stride=C), :]
        hi = w_scr[pl.ds(16 + k, C, stride=C), :]
        gwo_ref[k, 0:C, :] = jnp.where(core == 0, lo, hi)
        gwx_ref[k, 0:C, :] = jnp.where(core == 0, hi, lo)
        gwo_ref[k, C : C + 8, :] = bias
        gwx_ref[k, C : C + 8, :] = bias


def finish_kernel(oh_ref, ol_ref, w_ref, b_ref, goh_ref, gol_ref, bh_ref, bl_ref, p_ref, gl_ref, wp_scr, s_scr):
    core = core_index()
    load_weight(w_ref, wp_scr)
    wth, wtl = split(wp_scr[...].T)
    wcat = jnp.concatenate([wth, wtl], axis=0)

    @pl.loop(0, 4)
    def _(n):
        cols = pl.ds(pl.multiple_of(n * 256, 256), 256)
        r = dot(wcat, oh_ref[:, cols])
        r = r[:Z] + r[Z:] + dot(wth, ol_ref[:, cols])
        p_ref[cols, :] = (r * (1.0 / S)).T + b_ref[...]

    bh = bh_ref[...]
    bcat = jnp.concatenate([bh, bl_ref[...]], axis=1)
    r = dot(goh_ref[...], bcat)
    r = (r[:, :S] + r[:, S:] + dot(gol_ref[...], bh)) * (1.0 / S)
    s_scr[...] = r.T
    for k in range(16):
        own = s_scr[4 * k : 4 * k + 4, :]
        other = s_scr[64 + 4 * k : 68 + 4 * k, :]
        gl_ref[8 * k : 8 * k + 4, :] = jnp.where(core == 0, own, other)
        gl_ref[8 * k + 4 : 8 * k + 8, :] = jnp.where(core == 0, other, own)


def join_kernel(own_ref, other_ref, out_ref):
    core = core_index()
    for k in range(16):
        own = own_ref[k]
        other = other_ref[k]
        out_ref[C * k : C * k + C, :] = jnp.where(core == 0, own, other)
        out_ref[512 + C * k : 512 + C * k + C, :] = jnp.where(core == 0, other, own)


def call(kernel, outs, scratch, flops, nbytes):
    vmem = pl.BlockSpec(memory_space=pltpu.VMEM)

    def run(*args):
        return pl.pallas_call(
            kernel,
            out_shape=[jax.ShapeDtypeStruct(s, d) for s, d in outs],
            in_specs=[vmem] * len(args),
            out_specs=[vmem] * len(outs),
            scratch_shapes=[pltpu.VMEM(s, d) for s, d in scratch],
            cost_estimate=pl.CostEstimate(flops=flops, bytes_accessed=nbytes, transcendentals=0),
            compiler_params=pltpu.CompilerParams(vmem_limit_bytes=40 << 20),
        )(*args)

    return run


grad_outer_call = call(grad_outer_kernel, [((IC, JE), BF16)] * 2, [((CE, Z), F32), ((CE, 256), F32)], 10**9, 5 << 20)
grad_right_call = call(grad_right_kernel, [((16, 4, JE), F32)] * 2, [((S, IC), F32), ((JE, S), F32)], 10**9, 5 << 20)
outer_call = call(
    outer_kernel,
    [((CE, IJ), BF16)] * 2 + [((JE, S), BF16)] * 2 + [((16, 40, Z), F32)] * 2,
    [((S, IC), F32), ((S, JE), F32), ((JE, S), F32), ((IC, 256), F32), ((CE, Z), F32)],
    2 * 10**9, 7 << 20)
finish_call = call(finish_kernel, [((IJ, Z), F32), ((S, IC), F32)], [((CE, Z), F32), ((S, IC), F32)], 2 * 10**9, 9 << 20)
join_call = call(join_kernel, [((CE, Z), F32)], [], 10**5, 1 << 20)


def rid(z, y, c):
    return (z * 4 + y) * 2 + c


CORE = [(r, r ^ 1) for r in range(32)]
YZ = [[rid(z, y, c) for z in range(4) for y in range(4)] for c in range(2)]
XY = [[rid(z, y, c) * 8 + h * 4 + x for y in range(4) for x in range(4)] for z in range(4) for h in range(2) for c in range(2)]
Z8 = [[rid(z, y, c) * 8 + h * 4 + x for z in range(4) for h in range(2)] for y in range(4) for x in range(4) for c in range(2)]
BOTH = ("row", "col")


def spread(x, n, axis, groups=None):
    copies = jnp.broadcast_to(x[None], (n,) + x.shape)
    return lax.all_to_all(copies, axis, 0, 0, axis_index_groups=groups)


def body(left, right, w_out, b_out, pair_grad):
    g = pair_grad.reshape(IJ, Z)
    goh, gol = grad_outer_call(g, w_out)
    left_all = spread(left, 8, "col").reshape(S, IC)
    right_own = spread(right, 16, "row", YZ)
    right_other = lax.ppermute(right_own, "row", CORE)
    gr_own, gr_other = grad_right_call(left_all, goh, gol)
    oh, ol, bh, bl, gw_own, gw_other = outer_call(left_all, right_own, right_other, g)
    gw = gw_own + lax.ppermute(gw_other, "row", CORE)
    gw = jnp.sum(lax.all_to_all(gw, BOTH, 0, 0, axis_index_groups=XY), axis=0)
    gw = jnp.sum(spread(gw, 8, BOTH, Z8), axis=0) * (1.0 / 512)
    grad_bias = gw[C]
    gw_own = spread(gw[:C], 16, BOTH, XY)
    gw_other = lax.ppermute(gw_own, "row", CORE)
    (grad_weight,) = join_call(gw_own, gw_other)
    pair_out, gl = finish_call(oh, ol, w_out, b_out.reshape(1, Z), goh, gol, bh, bl)
    gr = gr_own + lax.ppermute(gr_other, "row", CORE)
    grad_right = jnp.sum(lax.all_to_all(gr, "row", 0, 0, axis_index_groups=YZ), axis=0)
    grad_left = jnp.sum(lax.all_to_all(gl.reshape(8, 16, IC), "col", 0, 0), axis=0)
    return (pair_out.reshape(TI, TJ, Z), grad_left, grad_right, grad_weight, grad_bias)


def solution(mesh):
    placed = (P("col", "row"), P("row", "col"), P(), P(), P("row", "col", None))
    return jax.shard_map(
        body,
        mesh=mesh,
        in_specs=placed,
        out_specs=(P("row", "col", None), P("col", "row"), P("row", "col"), P(), P()),
        check_vma=False,
    )
```

```python
import jax
import jax.numpy as jnp
from jax import lax
from jax.experimental import pallas as pl
from jax.experimental.pallas import tpu as pltpu
from jax.sharding import PartitionSpec as P

C = 32
Z = 128
S = 128
TI = 16
TJ = 64
IC = TI * C
JE = TJ * C
IJ = TI * TJ
CE = C * C
F32 = jnp.float32
BF16 = jnp.bfloat16
NT = (((1,), (1,)), ((), ()))
NN = (((1,), (0,)), ((), ()))


def split(x):
    hi = x.astype(BF16)
    return hi, (x - hi.astype(F32)).astype(BF16)


def dot(x, y, dims=NN):
    return lax.dot_general(x, y, dims, preferred_element_type=F32)


def half_swap(x0, x1):
    lane = lax.broadcasted_iota(jnp.int32, x0.shape, 1)
    low = lane < 64
    r0 = pltpu.roll(x0, 64, 1)
    r1 = pltpu.roll(x1, 64, 1)
    return jnp.where(low, x0, r1), jnp.where(low, r0, x1)


def core_index():
    return lax.rem(lax.axis_index("row"), 2)


def load_left(near_ref, far_ref, a_scr):
    core = core_index()
    col = lax.axis_index("col")
    for ref, half in ((near_ref, col // 4), (far_ref, 1 - col // 4)):
        for p in range(4):
            q = half * 4 + lax.rem(col + 4 - p, 4)
            x = ref[p]
            lo = jnp.concatenate([x[0:4], x[8:12]], axis=0)
            hi = jnp.concatenate([x[4:8], x[12:16]], axis=0)
            a_scr[pl.ds(pl.multiple_of(q * 8, 8), 8), :] = jnp.where(core == 0, lo, hi)
            a_scr[pl.ds(pl.multiple_of(64 + q * 8, 8), 8), :] = jnp.where(core == 0, hi, lo)


def load_weight(w_ref, wp_scr):
    for e in range(C):
        wp_scr[C * e : C * e + C, :] = w_ref[pl.ds(e, C, stride=C), :]


def grad_outer_kernel(g_ref, w_ref, goh_ref, gol_ref, wp_scr, wc_scr, r_scr):
    @pl.when(pl.program_id(0) == 0)
    def _():
        load_weight(w_ref, wp_scr)
        wh, wl = split(wp_scr[...])
        wc_scr[:, 0:Z] = wh
        wc_scr[:, Z : 2 * Z] = wl

    gh, gl = split(g_ref[...])
    r_scr[...] = dot(wc_scr[...], jnp.concatenate([gh, gh], axis=1), NT) + dot(wc_scr[:, 0:Z], gl, NT)
    for ip in range(2):
        for ep in range(16):
            x0 = r_scr[64 * ep : 64 * ep + 32, 128 * ip : 128 * ip + 128]
            x1 = r_scr[64 * ep + 32 : 64 * ep + 64, 128 * ip : 128 * ip + 128]
            for k, y in enumerate(half_swap(x0, x1)):
                hi, lo = split(y)
                row = (2 * ip + k) * C
                goh_ref[row : row + C, 128 * ep : 128 * ep + 128] = hi
                gol_ref[row : row + C, 128 * ep : 128 * ep + 128] = lo


def grad_right_kernel(near_ref, far_ref, goh_ref, gol_ref, own_ref, other_ref, a_scr, ac_scr, t_scr):
    n = pl.program_id(0)

    @pl.when(n == 0)
    def _():
        load_left(near_ref, far_ref, a_scr)
        ah, al = split(a_scr[...])
        ac_scr[0:S, :] = ah
        ac_scr[S : 2 * S, :] = al

    r = dot(ac_scr[...], goh_ref[...])
    r = r[:S] + r[S:] + dot(ac_scr[0:S, :], gol_ref[...])
    t_scr[pl.ds(pl.multiple_of(n * 512, 512), 512), :] = (r * (1.0 / S)).T

    @pl.when(n == 3)
    def _():
        row = lax.axis_index("row") // 2
        y = lax.rem(row, 4)
        z = row // 4
        for m in range(16):
            block = jnp.concatenate([t_scr[pl.ds(4 * m + q, C, stride=TJ), :] for q in range(4)], axis=0)
            block = block.T
            for k in range(16):
                yy = lax.rem(k % 4 + 4 - y, 4)
                zz = lax.rem(k // 4 + 4 - z, 4)
                own_ref[yy, zz, :, 128 * m : 128 * m + 128] = block[4 * k : 4 * k + 4]
                other_ref[yy, zz, :, 128 * m : 128 * m + 128] = block[64 + 4 * k : 68 + 4 * k]


def outer_kernel(near_ref, far_ref, own_ref, other_ref, g_ref, oh_ref, ol_ref, bh_ref, bl_ref, gwo_ref, gwx_ref,
                 a_scr, at_scr, b_scr, t_scr, r_scr, gc_scr, w_scr):
    n = pl.program_id(0)

    @pl.when(n == 0)
    def _():
        load_left(near_ref, far_ref, a_scr)
        ath, atl = split(a_scr[...].T)
        at_scr[:, 0:S] = ath
        at_scr[:, S : 2 * S] = atl
        for k in range(16):
            b_scr[4 * k : 4 * k + 4, :] = own_ref[k]
            b_scr[64 + 4 * k : 68 + 4 * k, :] = other_ref[k]
        for m in range(16):
            t_scr[128 * m : 128 * m + 128, :] = b_scr[:, 128 * m : 128 * m + 128].T
        gh, gl = split(g_ref[...])
        gc_scr[:, 0:Z] = gh
        gc_scr[:, Z : 2 * Z] = gl

    for e in range(8):
        hi, lo = split(t_scr[pl.ds(8 * n + e, TJ, stride=C), :])
        bh_ref[TJ * e : TJ * e + TJ, :] = hi
        bl_ref[TJ * e : TJ * e + TJ, :] = lo
    for h in range(2):
        bh = bh_ref[256 * h : 256 * h + 256, :]
        bl = bl_ref[256 * h : 256 * h + 256, :]
        r_scr[h] = dot(at_scr[...], jnp.concatenate([bh, bh], axis=1), NT) + dot(at_scr[:, 0:S], bl, NT)
        for ep in range(2):
            for ip in range(8):
                x0 = r_scr[h, 64 * ip : 64 * ip + 32, 128 * ep : 128 * ep + 128]
                x1 = r_scr[h, 64 * ip + 32 : 64 * ip + 64, 128 * ep : 128 * ep + 128]
                for k, y in enumerate(half_swap(x0, x1)):
                    hi, lo = split(y)
                    row = (4 * h + 2 * ep + k) * C
                    oh_ref[row : row + C, 128 * ip : 128 * ip + 128] = hi
                    ol_ref[row : row + C, 128 * ip : 128 * ip + 128] = lo
    r = dot(oh_ref[...], gc_scr[...])
    rows = pl.ds(pl.multiple_of(n * 256, 256), 256)
    w_scr[rows, :] = (r[:, :Z] + r[:, Z:] + dot(ol_ref[...], gc_scr[:, 0:Z])) * (1.0 / S)

    @pl.when(n == 3)
    def _():
        core = core_index()
        bias = jnp.broadcast_to(jnp.sum(g_ref[...], axis=0, keepdims=True), (8, Z))
        for k in range(16):
            lo = w_scr[pl.ds(k, C, stride=C), :]
            hi = w_scr[pl.ds(16 + k, C, stride=C), :]
            gwo_ref[k, 0:C, :] = jnp.where(core == 0, lo, hi)
            gwx_ref[k, 0:C, :] = jnp.where(core == 0, hi, lo)
            gwo_ref[k, C : C + 8, :] = bias
            gwx_ref[k, C : C + 8, :] = bias


def finish_kernel(oh_ref, ol_ref, w_ref, b_ref, goh_ref, gol_ref, bh_ref, bl_ref, p_ref, gl_ref, wp_scr, wc_scr, acc_scr, s_scr):
    n = pl.program_id(0)

    @pl.when(n == 0)
    def _():
        load_weight(w_ref, wp_scr)
        wth, wtl = split(wp_scr[...].T)
        wc_scr[0:Z, :] = wth
        wc_scr[Z : 2 * Z, :] = wtl
        acc_scr[...] = jnp.zeros_like(acc_scr)

    r = dot(wc_scr[...], oh_ref[...])
    r = r[:Z] + r[Z:] + dot(wc_scr[0:Z, :], ol_ref[...])
    p_ref[...] = (r * (1.0 / S)).T + b_ref[...]
    bh = bh_ref[...]
    r = dot(goh_ref[...], jnp.concatenate([bh, bl_ref[...]], axis=1))
    acc_scr[...] += r[:, :S] + r[:, S:] + dot(gol_ref[...], bh)

    @pl.when(n == 3)
    def _():
        core = core_index()
        col = lax.axis_index("col")
        s_scr[...] = (acc_scr[...] * (1.0 / S)).T
        for q in range(8):
            own = s_scr[8 * q : 8 * q + 8, :]
            other = s_scr[64 + 8 * q : 72 + 8 * q, :]
            lo = jnp.where(core == 0, own, other)
            hi = jnp.where(core == 0, other, own)
            xx = lax.rem(q % 4 + 4 - lax.rem(col, 4), 4)
            zz = lax.rem(q // 4 + 2 - col // 4, 2)
            gl_ref[xx, zz, 0:8, :] = jnp.concatenate([lo[0:4], hi[0:4]], axis=0)
            gl_ref[xx, zz, 8:16, :] = jnp.concatenate([lo[4:8], hi[4:8]], axis=0)


def sum_spread_kernel(x_ref, out_ref):
    total = x_ref[0]
    for k in range(1, x_ref.shape[0]):
        total = total + x_ref[k]
    for k in range(out_ref.shape[0]):
        out_ref[k] = total


def sum_final_kernel(x_ref, out_ref, bias_ref):
    total = x_ref[0]
    for k in range(1, x_ref.shape[0]):
        total = total + x_ref[k]
    total = total * (1.0 / 512)
    for k in range(out_ref.shape[0]):
        out_ref[k] = total[:C]
    bias_ref[...] = total[C : C + 1]


def join_kernel(own_ref, other_ref, out_ref):
    core = core_index()
    for k in range(16):
        own = own_ref[k]
        other = other_ref[k]
        out_ref[C * k : C * k + C, :] = jnp.where(core == 0, own, other)
        out_ref[512 + C * k : 512 + C * k + C, :] = jnp.where(core == 0, other, own)


def whole(shape):
    return pl.BlockSpec(shape, lambda n: (0,) * len(shape))


def rows_of(shape):
    return pl.BlockSpec(shape, lambda n: (n, 0))


def cols_of(shape):
    return pl.BlockSpec(shape, lambda n: (0, n))


def call(kernel, ins, outs, scratch, flops, nbytes, steps=4):
    return pl.pallas_call(
        kernel,
        grid=(steps,),
        in_specs=ins,
        out_specs=[spec for _, _, spec in outs],
        out_shape=[pltpu.HBM(s, d) if d == BF16 else jax.ShapeDtypeStruct(s, d) for s, d, _ in outs],
        scratch_shapes=[pltpu.VMEM(s, d) for s, d in scratch],
        cost_estimate=pl.CostEstimate(flops=flops, bytes_accessed=nbytes, transcendentals=0),
        compiler_params=pltpu.CompilerParams(vmem_limit_bytes=40 << 20),
    )


LEFT = whole((4, 16, IC))
RIGHT = whole((16, 4, JE))
WHOLE_G = whole((IJ, Z))
WEIGHT = whole((CE, Z))
grad_outer_call = call(
    grad_outer_kernel,
    [rows_of((256, Z)), WEIGHT],
    [((IC, JE), BF16, rows_of((128, JE)))] * 2,
    [((CE, Z), F32), ((CE, 2 * Z), BF16), ((CE, 256), F32)],
    10**9, 5 << 20)
grad_right_call = call(
    grad_right_kernel,
    [LEFT, LEFT, cols_of((IC, 512)), cols_of((IC, 512))],
    [((4, 4, 4, JE), F32, whole((4, 4, 4, JE)))] * 2,
    [((S, IC), F32), ((2 * S, IC), BF16), ((JE, S), F32)],
    10**9, 5 << 20)
outer_call = call(
    outer_kernel,
    [LEFT, LEFT, RIGHT, RIGHT, WHOLE_G],
    [((CE, IJ), BF16, rows_of((256, IJ)))] * 2 + [((JE, S), BF16, rows_of((512, S)))] * 2
    + [((16, 40, Z), F32, whole((16, 40, Z)))] * 2,
    [((S, IC), F32), ((IC, 2 * S), BF16), ((S, JE), F32), ((JE, S), F32), ((2, IC, 256), F32), ((IJ, 2 * Z), BF16), ((CE, Z), F32)],
    2 * 10**9, 7 << 20)
finish_call = call(
    finish_kernel,
    [cols_of((CE, 256))] * 2 + [WEIGHT, whole((1, Z))] + [cols_of((IC, 512))] * 2 + [rows_of((512, S))] * 2,
    [((IJ, Z), F32, rows_of((256, Z))), ((4, 2, 16, IC), F32, whole((4, 2, 16, IC)))],
    [((CE, Z), F32), ((2 * Z, CE), BF16), ((IC, S), F32), ((S, IC), F32)],
    2 * 10**9, 9 << 20)
join_call = call(join_kernel, [whole((16, C, Z))] * 2, [((CE, Z), F32, WEIGHT)], [], 10**5, 1 << 20, 1)
spread_call = call(sum_spread_kernel, [whole((16, 40, Z))], [((8, 40, Z), F32, whole((8, 40, Z)))], [], 10**5, 1 << 19, 1)
final_call = call(
    sum_final_kernel,
    [whole((8, 40, Z))],
    [((16, C, Z), F32, whole((16, C, Z))), ((1, Z), F32, whole((1, Z)))],
    [], 10**5, 1 << 19, 1)


def rid(z, y, c):
    return (z * 4 + y) * 2 + c


CORE = [(r, r ^ 1) for r in range(32)]
YZ = [[rid(z, y, c) for z in range(4) for y in range(4)] for c in range(2)]
XY = [[rid(z, y, c) * 8 + h * 4 + x for y in range(4) for x in range(4)] for z in range(4) for h in range(2) for c in range(2)]
Z8 = [[rid(z, y, c) * 8 + h * 4 + x for z in range(4) for h in range(2)] for y in range(4) for x in range(4) for c in range(2)]
BOTH = ("row", "col")
R4 = range(4)
Y_PERMS = [[(rid(z, y, c), rid(z, (y + k) % 4, c)) for z in R4 for y in R4 for c in range(2)] for k in (1, 2, 3)]
Z_PERMS = [[(rid(z, y, c), rid((z + k) % 4, y, c)) for z in R4 for y in R4 for c in range(2)] for k in (1, 2, 3)]
X_PERMS = [[(h * 4 + x, h * 4 + (x + k) % 4) for h in range(2) for x in R4] for k in (1, 2, 3)]
H_PERM = [(q, q ^ 4) for q in range(8)]


def spread(x, n, axis, groups=None):
    copies = jnp.broadcast_to(x[None], (n,) + x.shape)
    return lax.all_to_all(copies, axis, 0, 0, axis_index_groups=groups)


def body(left, right, w_out, b_out, pair_grad):
    g = pair_grad.reshape(IJ, Z)
    right_own = spread(right, 16, "row", YZ)
    left_near = jnp.stack([left] + [lax.ppermute(left, "col", p) for p in X_PERMS])
    left_far = lax.ppermute(left_near, "col", H_PERM)
    goh, gol = grad_outer_call(g, w_out)
    right_other = lax.ppermute(right_own, "row", CORE)
    oh, ol, bh, bl, gw_own, gw_other = outer_call(left_near, left_far, right_own, right_other, g)
    gw = gw_own + lax.ppermute(gw_other, "row", CORE)
    gw = lax.all_to_all(gw, BOTH, 0, 0, axis_index_groups=XY)
    (gw,) = spread_call(gw)
    gw = lax.all_to_all(gw, BOTH, 0, 0, axis_index_groups=Z8)
    gw, grad_bias = final_call(gw)
    gw_own = lax.all_to_all(gw, BOTH, 0, 0, axis_index_groups=XY)
    gw_other = lax.ppermute(gw_own, "row", CORE)
    (grad_weight,) = join_call(gw_own, gw_other)
    gr_own, gr_other = grad_right_call(left_near, left_far, goh, gol)
    gr = gr_own + lax.ppermute(gr_other, "row", CORE)
    gr = gr[0] + sum(lax.ppermute(gr[k + 1], "row", p) for k, p in enumerate(Y_PERMS))
    grad_right = gr[0] + sum(lax.ppermute(gr[k + 1], "row", p) for k, p in enumerate(Z_PERMS))
    pair_out, gl = finish_call(oh, ol, w_out, b_out.reshape(1, Z), goh, gol, bh, bl)
    gl = gl[0] + sum(lax.ppermute(gl[k + 1], "col", p) for k, p in enumerate(X_PERMS))
    grad_left = gl[0] + lax.ppermute(gl[1], "col", H_PERM)
    return (pair_out.reshape(TI, TJ, Z), grad_left, grad_right, grad_weight, grad_bias.reshape(Z))


def solution(mesh):
    placed = (P("col", "row"), P("row", "col"), P(), P(), P("row", "col", None))
    return jax.shard_map(
        body,
        mesh=mesh,
        in_specs=placed,
        out_specs=(P("row", "col", None), P("col", "row"), P("row", "col"), P(), P()),
        check_vma=False,
    )
```

```python
import jax
import jax.numpy as jnp
from jax import lax
from jax.experimental import pallas as pl
from jax.experimental.pallas import tpu as pltpu
from jax.sharding import PartitionSpec as P


C = 32
Z = 128
S = 128
TI = 16
TJ = 64
IC = TI * C
JE = TJ * C
IJ = TI * TJ
CE = C * C
F32 = jnp.float32
BF16 = jnp.bfloat16
NT = (((1,), (1,)), ((), ()))
NN = (((1,), (0,)), ((), ()))


def split(x):
    hi = x.astype(BF16)
    return hi, (x - hi.astype(F32)).astype(BF16)


def dot(x, y, dims=NN):
    return lax.dot_general(x, y, dims, preferred_element_type=F32)


def half_swap(x0, x1):
    lane = lax.broadcasted_iota(jnp.int32, x0.shape, 1)
    low = lane < 64
    r0 = pltpu.roll(x0, 64, 1)
    r1 = pltpu.roll(x1, 64, 1)
    return jnp.where(low, x0, r1), jnp.where(low, r0, x1)


def core_index():
    return lax.rem(lax.axis_index("row"), 2)


def load_left(piece_refs, a_scr):
    core = core_index()
    col = lax.axis_index("col")
    for p, ref in enumerate(piece_refs):
        for h, half in ((0, col // 4), (1, 1 - col // 4)):
            q = half * 4 + lax.rem(col + 4 - p, 4)
            x = ref[h]
            lo = jnp.concatenate([x[0:4], x[8:12]], axis=0)
            hi = jnp.concatenate([x[4:8], x[12:16]], axis=0)
            a_scr[pl.ds(pl.multiple_of(q * 8, 8), 8), :] = jnp.where(core == 0, lo, hi)
            a_scr[pl.ds(pl.multiple_of(64 + q * 8, 8), 8), :] = jnp.where(core == 0, hi, lo)


def load_weight(w_ref, wp_scr):
    for e in range(C):
        wp_scr[C * e : C * e + C, :] = w_ref[pl.ds(e, C, stride=C), :]


def grad_outer_kernel(g_ref, w_ref, goh_ref, gol_ref, wp_scr, wc_scr, r_scr):
    @pl.when(pl.program_id(0) == 0)
    def _():
        load_weight(w_ref, wp_scr)
        wh, wl = split(wp_scr[...])
        wc_scr[:, 0:Z] = wh
        wc_scr[:, Z : 2 * Z] = wl

    gh, gl = split(g_ref[...])
    r_scr[...] = dot(wc_scr[...], jnp.concatenate([gh, gh], axis=1), NT) + dot(wc_scr[:, 0:Z], gl, NT)
    for ip in range(2):
        for ep in range(16):
            x0 = r_scr[64 * ep : 64 * ep + 32, 128 * ip : 128 * ip + 128]
            x1 = r_scr[64 * ep + 32 : 64 * ep + 64, 128 * ip : 128 * ip + 128]
            for k, y in enumerate(half_swap(x0, x1)):
                hi, lo = split(y)
                row = (2 * ip + k) * C
                goh_ref[row : row + C, 128 * ep : 128 * ep + 128] = hi
                gol_ref[row : row + C, 128 * ep : 128 * ep + 128] = lo


def grad_right_kernel(l0_ref, l1_ref, l2_ref, l3_ref, goh_ref, gol_ref, own_ref, other_ref, a_scr, ac_scr, t_scr):
    n = pl.program_id(0)

    @pl.when(n == 0)
    def _():
        load_left((l0_ref, l1_ref, l2_ref, l3_ref), a_scr)
        ah, al = split(a_scr[...])
        ac_scr[0:S, :] = ah
        ac_scr[S : 2 * S, :] = al

    r = dot(ac_scr[...], goh_ref[...])
    r = r[:S] + r[S:] + dot(ac_scr[0:S, :], gol_ref[...])
    t_scr[pl.ds(pl.multiple_of(n * 512, 512), 512), :] = (r * (1.0 / S)).T

    @pl.when(n == 3)
    def _():
        row = lax.axis_index("row") // 2
        y = lax.rem(row, 4)
        z = row // 4
        for m in range(16):
            block = jnp.concatenate([t_scr[pl.ds(4 * m + q, C, stride=TJ), :] for q in range(4)], axis=0)
            block = block.T
            for k in range(16):
                yy = lax.rem(k % 4 + 4 - y, 4)
                zz = lax.rem(k // 4 + 4 - z, 4)
                own_ref[yy, zz, :, 128 * m : 128 * m + 128] = block[4 * k : 4 * k + 4]
                other_ref[yy, zz, :, 128 * m : 128 * m + 128] = block[64 + 4 * k : 68 + 4 * k]


def outer_kernel(l0_ref, l1_ref, l2_ref, l3_ref, own_ref, other_ref, g_ref, oh_ref, ol_ref, bh_ref, bl_ref, gwo_ref, gwx_ref,
                 a_scr, at_scr, b_scr, t_scr, r_scr, gc_scr, w_scr):
    n = pl.program_id(0)

    @pl.when(n == 0)
    def _():
        load_left((l0_ref, l1_ref, l2_ref, l3_ref), a_scr)
        ath, atl = split(a_scr[...].T)
        at_scr[:, 0:S] = ath
        at_scr[:, S : 2 * S] = atl
        for k in range(16):
            b_scr[4 * k : 4 * k + 4, :] = own_ref[k]
            b_scr[64 + 4 * k : 68 + 4 * k, :] = other_ref[k]
        for m in range(16):
            t_scr[128 * m : 128 * m + 128, :] = b_scr[:, 128 * m : 128 * m + 128].T
        gh, gl = split(g_ref[...])
        gc_scr[:, 0:Z] = gh
        gc_scr[:, Z : 2 * Z] = gl

    for e in range(8):
        hi, lo = split(t_scr[pl.ds(8 * n + e, TJ, stride=C), :])
        bh_ref[TJ * e : TJ * e + TJ, :] = hi
        bl_ref[TJ * e : TJ * e + TJ, :] = lo
    for h in range(2):
        bh = bh_ref[256 * h : 256 * h + 256, :]
        bl = bl_ref[256 * h : 256 * h + 256, :]
        r_scr[h] = dot(at_scr[...], jnp.concatenate([bh, bh], axis=1), NT) + dot(at_scr[:, 0:S], bl, NT)
        for ep in range(2):
            for ip in range(8):
                x0 = r_scr[h, 64 * ip : 64 * ip + 32, 128 * ep : 128 * ep + 128]
                x1 = r_scr[h, 64 * ip + 32 : 64 * ip + 64, 128 * ep : 128 * ep + 128]
                for k, y in enumerate(half_swap(x0, x1)):
                    hi, lo = split(y)
                    row = (4 * h + 2 * ep + k) * C
                    oh_ref[row : row + C, 128 * ip : 128 * ip + 128] = hi
                    ol_ref[row : row + C, 128 * ip : 128 * ip + 128] = lo
    r = dot(oh_ref[...], gc_scr[...])
    rows = pl.ds(pl.multiple_of(n * 256, 256), 256)
    w_scr[rows, :] = (r[:, :Z] + r[:, Z:] + dot(ol_ref[...], gc_scr[:, 0:Z])) * (1.0 / S)

    @pl.when(n == 3)
    def _():
        core = core_index()
        bias = jnp.broadcast_to(jnp.sum(g_ref[...], axis=0, keepdims=True), (8, Z))
        for k in range(16):
            lo = w_scr[pl.ds(k, C, stride=C), :]
            hi = w_scr[pl.ds(16 + k, C, stride=C), :]
            gwo_ref[k, 0:C, :] = jnp.where(core == 0, lo, hi)
            gwx_ref[k, 0:C, :] = jnp.where(core == 0, hi, lo)
            gwo_ref[k, C : C + 8, :] = bias
            gwx_ref[k, C : C + 8, :] = bias


def pair_kernel(oh_ref, ol_ref, w_ref, b_ref, p_ref, wp_scr, wc_scr):
    @pl.when(pl.program_id(0) == 0)
    def _():
        load_weight(w_ref, wp_scr)
        wth, wtl = split(wp_scr[...].T)
        wc_scr[0:Z, :] = wth
        wc_scr[Z : 2 * Z, :] = wtl

    r = dot(wc_scr[...], oh_ref[...])
    r = r[:Z] + r[Z:] + dot(wc_scr[0:Z, :], ol_ref[...])
    p_ref[...] = (r * (1.0 / S)).T + b_ref[...]


def grad_left_kernel(goh_ref, gol_ref, bh_ref, bl_ref, gl_ref, acc_scr, s_scr):
    n = pl.program_id(0)

    @pl.when(n == 0)
    def _():
        acc_scr[...] = jnp.zeros_like(acc_scr)

    bh = bh_ref[...]
    r = dot(goh_ref[...], jnp.concatenate([bh, bl_ref[...]], axis=1))
    acc_scr[...] += r[:, :S] + r[:, S:] + dot(gol_ref[...], bh)

    @pl.when(n == 3)
    def _():
        core = core_index()
        col = lax.axis_index("col")
        s_scr[...] = (acc_scr[...] * (1.0 / S)).T
        for q in range(8):
            own = s_scr[8 * q : 8 * q + 8, :]
            other = s_scr[64 + 8 * q : 72 + 8 * q, :]
            lo = jnp.where(core == 0, own, other)
            hi = jnp.where(core == 0, other, own)
            xx = lax.rem(q % 4 + 4 - lax.rem(col, 4), 4)
            zz = lax.rem(q // 4 + 2 - col // 4, 2)
            gl_ref[xx, zz, 0:8, :] = jnp.concatenate([lo[0:4], hi[0:4]], axis=0)
            gl_ref[xx, zz, 8:16, :] = jnp.concatenate([lo[4:8], hi[4:8]], axis=0)


def copies_kernel(x_ref, out_ref):
    for k in range(out_ref.shape[0]):
        out_ref[k] = x_ref[...]


def sum_spread_kernel(x_ref, out_ref):
    total = x_ref[0]
    for k in range(1, x_ref.shape[0]):
        total = total + x_ref[k]
    for k in range(out_ref.shape[0]):
        out_ref[k] = total


def sum_final_kernel(x_ref, out_ref, bias_ref):
    total = x_ref[0]
    for k in range(1, x_ref.shape[0]):
        total = total + x_ref[k]
    total = total * (1.0 / 512)
    for k in range(out_ref.shape[0]):
        out_ref[k] = total[:C]
    bias_ref[...] = total[C : C + 1]


def join_kernel(own_ref, other_ref, r0_ref, r1_ref, r2_ref, r3_ref, l0_ref, l1_ref, w_ref, gr_ref, gl_ref):
    core = core_index()
    for k in range(16):
        own = own_ref[k]
        other = other_ref[k]
        w_ref[C * k : C * k + C, :] = jnp.where(core == 0, own, other)
        w_ref[512 + C * k : 512 + C * k + C, :] = jnp.where(core == 0, other, own)
    gr_ref[...] = (r0_ref[0] + r1_ref[...]) + (r2_ref[...] + r3_ref[...])
    gl_ref[...] = l0_ref[0] + l1_ref[...]


def whole(shape):
    return pl.BlockSpec(shape, lambda n: (0,) * len(shape))


def rows_of(shape):
    return pl.BlockSpec(shape, lambda n: (n, 0))


def cols_of(shape):
    return pl.BlockSpec(shape, lambda n: (0, n))


def call(kernel, ins, outs, scratch, flops, nbytes, steps=4, limit=40):
    return pl.pallas_call(
        kernel,
        grid=(steps,),
        in_specs=ins,
        out_specs=[spec for _, _, spec in outs],
        out_shape=[pltpu.HBM(s, d) if d == BF16 else jax.ShapeDtypeStruct(s, d) for s, d, _ in outs],
        scratch_shapes=[pltpu.VMEM(s, d) for s, d in scratch],
        cost_estimate=pl.CostEstimate(flops=flops, bytes_accessed=nbytes, transcendentals=0),
        compiler_params=pltpu.CompilerParams(vmem_limit_bytes=limit << 20),
    )


LEFT = whole((2, 16, IC))
RIGHT = whole((16, 4, JE))
WHOLE_G = whole((IJ, Z))
WEIGHT = whole((CE, Z))
grad_outer_call = call(
    grad_outer_kernel,
    [rows_of((256, Z)), WEIGHT],
    [((IC, JE), BF16, rows_of((128, JE)))] * 2,
    [((CE, Z), F32), ((CE, 2 * Z), BF16), ((CE, 256), F32)],
    10**9, 5 << 20)
grad_right_call = call(
    grad_right_kernel,
    [LEFT, LEFT, LEFT, LEFT, cols_of((IC, 512)), cols_of((IC, 512))],
    [((4, 4, 4, JE), F32, whole((4, 4, 4, JE)))] * 2,
    [((S, IC), F32), ((2 * S, IC), BF16), ((JE, S), F32)],
    10**9, 5 << 20)
outer_call = call(
    outer_kernel,
    [LEFT, LEFT, LEFT, LEFT, RIGHT, RIGHT, WHOLE_G],
    [((CE, IJ), BF16, rows_of((256, IJ)))] * 2 + [((JE, S), BF16, rows_of((512, S)))] * 2
    + [((16, 40, Z), F32, whole((16, 40, Z)))] * 2,
    [((S, IC), F32), ((IC, 2 * S), BF16), ((S, JE), F32), ((JE, S), F32), ((2, IC, 256), F32), ((IJ, 2 * Z), BF16), ((CE, Z), F32)],
    2 * 10**9, 7 << 20)
pair_call = call(
    pair_kernel,
    [cols_of((CE, 256))] * 2 + [WEIGHT, whole((1, Z))],
    [((IJ, Z), F32, rows_of((256, Z)))],
    [((CE, Z), F32), ((2 * Z, CE), BF16)],
    10**9, 5 << 20)
grad_left_call = call(
    grad_left_kernel,
    [cols_of((IC, 512))] * 2 + [rows_of((512, S))] * 2,
    [((4, 2, 16, IC), F32, whole((4, 2, 16, IC)))],
    [((IC, S), F32), ((S, IC), F32)],
    10**9, 6 << 20)
join_call = call(
    join_kernel,
    [whole((16, C, Z))] * 2 + [whole((4, 4, JE))] + [whole((4, JE))] * 3 + [whole((2, 16, IC)), whole((16, IC))],
    [((CE, Z), F32, WEIGHT), ((4, JE), F32, whole((4, JE))), ((16, IC), F32, whole((16, IC)))],
    [], 10**5, 1 << 20, 1, 8)
copies_call = call(copies_kernel, [whole((4, JE))], [((16, 4, JE), F32, RIGHT)], [], 10**5, 1 << 19, 1, 8)
spread_call = call(sum_spread_kernel, [whole((16, 40, Z))], [((8, 40, Z), F32, whole((8, 40, Z)))], [], 10**5, 1 << 19, 1, 8)
final_call = call(
    sum_final_kernel,
    [whole((8, 40, Z))],
    [((16, C, Z), F32, whole((16, C, Z))), ((1, Z), F32, whole((1, Z)))],
    [], 10**5, 1 << 19, 1, 8)


def rid(z, y, c):
    return (z * 4 + y) * 2 + c


CORE = [(r, r ^ 1) for r in range(32)]
YZ = [[rid(z, y, c) for z in range(4) for y in range(4)] for c in range(2)]
XY = [[rid(z, y, c) * 8 + h * 4 + x for y in range(4) for x in range(4)] for z in range(4) for h in range(2) for c in range(2)]
Z8 = [[rid(z, y, c) * 8 + h * 4 + x for z in range(4) for h in range(2)] for y in range(4) for x in range(4) for c in range(2)]
BOTH = ("row", "col")
R4 = range(4)
Y_PERMS = [[(rid(z, y, c), rid(z, (y + k) % 4, c)) for z in R4 for y in R4 for c in range(2)] for k in (1, 2, 3)]
Z_PERMS = [[(rid(z, y, c), rid((z + k) % 4, y, c)) for z in R4 for y in R4 for c in range(2)] for k in (1, 2, 3)]
X_PERMS = [[(h * 4 + x, h * 4 + (x + k) % 4) for h in range(2) for x in R4] for k in (1, 2, 3)]
H_PERM = [(q, q ^ 4) for q in range(8)]


def in_hbm(*xs):
    return [pltpu.with_memory_space_constraint(x, pltpu.HBM) for x in xs]


def body(left, right, w_out, b_out, pair_grad):
    tie = lax.optimization_barrier
    g = pair_grad.reshape(IJ, Z)
    left_far = lax.ppermute(left, "col", H_PERM)
    (copies,) = copies_call(right)
    right_own = lax.all_to_all(copies, "row", 0, 0, axis_index_groups=YZ)
    left_pair = jnp.stack([left, left_far])
    pieces = [left_pair] + [lax.ppermute(left_pair, "col", p) for p in X_PERMS]
    goh, gol = grad_outer_call(*in_hbm(g, w_out))
    right_other = lax.ppermute(right_own, "row", CORE)
    oh, ol, bh, bl, gw_own, gw_other = outer_call(*pieces, right_own, right_other, g)
    gw = gw_own + lax.ppermute(gw_other, "row", CORE)
    gw, goh, gol = tie((gw, goh, gol))
    gw = lax.all_to_all(gw, BOTH, 0, 0, axis_index_groups=XY)
    gr_own, gr_other = grad_right_call(*pieces, *in_hbm(goh, gol))
    gr = gr_own + lax.ppermute(gr_other, "row", CORE)
    (gl,) = grad_left_call(*in_hbm(goh, gol, bh, bl))
    (gw,) = spread_call(gw)
    gw, oh, ol = tie((gw, oh, ol))
    gr = gr[0] + sum(lax.ppermute(gr[k + 1], "row", p) for k, p in enumerate(Y_PERMS))
    gl = gl[0] + sum(lax.ppermute(gl[k + 1], "col", p) for k, p in enumerate(X_PERMS))
    gw = lax.all_to_all(gw, BOTH, 0, 0, axis_index_groups=Z8)
    (pair_out,) = pair_call(*in_hbm(oh, ol, w_out), b_out.reshape(1, Z))
    gw, grad_bias = final_call(gw)
    gr_parts = [lax.ppermute(gr[k + 1], "row", p) for k, p in enumerate(Z_PERMS)]
    gl_part = lax.ppermute(gl[1], "col", H_PERM)
    gw_own = lax.all_to_all(gw, BOTH, 0, 0, axis_index_groups=XY)
    gw_other = lax.ppermute(gw_own, "row", CORE)
    grad_weight, grad_right, grad_left = join_call(gw_own, gw_other, gr, *gr_parts, gl, gl_part)
    return (pair_out.reshape(TI, TJ, Z), grad_left, grad_right, grad_weight, grad_bias.reshape(Z))


def solution(mesh):
    placed = (P("col", "row"), P("row", "col"), P(), P(), P("row", "col", None))
    return jax.shard_map(
        body,
        mesh=mesh,
        in_specs=placed,
        out_specs=(P("row", "col", None), P("col", "row"), P("row", "col"), P(), P()),
        check_vma=False,
    )
```

```python
import jax
import jax.numpy as jnp
from jax import lax
from jax.experimental import pallas as pl
from jax.experimental.pallas import tpu as pltpu
from jax.sharding import PartitionSpec as P


C = 32
Z = 128
S = 128
TI = 16
TJ = 64
IC = TI * C
JE = TJ * C
IJ = TI * TJ
CE = C * C
F32 = jnp.float32
BF16 = jnp.bfloat16
NT = (((1,), (1,)), ((), ()))
NN = (((1,), (0,)), ((), ()))


def split(x):
    hi = x.astype(BF16)
    return hi, (x - hi.astype(F32)).astype(BF16)


def dot(x, y, dims=NN):
    return lax.dot_general(x, y, dims, preferred_element_type=F32)


def half_swap(x0, x1):
    lane = lax.broadcasted_iota(jnp.int32, x0.shape, 1)
    low = lane < 64
    r0 = pltpu.roll(x0, 64, 1)
    r1 = pltpu.roll(x1, 64, 1)
    return jnp.where(low, x0, r1), jnp.where(low, r0, x1)


def core_index():
    return lax.rem(lax.axis_index("row"), 2)


def load_left(piece_refs, a_scr):
    core = core_index()
    col = lax.axis_index("col")
    for p, ref in enumerate(piece_refs):
        for h, half in ((0, col // 4), (1, 1 - col // 4)):
            q = half * 4 + lax.rem(col + 4 - p, 4)
            x = ref[h]
            lo = jnp.concatenate([x[0:4], x[8:12]], axis=0)
            hi = jnp.concatenate([x[4:8], x[12:16]], axis=0)
            a_scr[pl.ds(pl.multiple_of(q * 8, 8), 8), :] = jnp.where(core == 0, lo, hi)
            a_scr[pl.ds(pl.multiple_of(64 + q * 8, 8), 8), :] = jnp.where(core == 0, hi, lo)


def load_weight(w_ref, wp_scr):
    for e in range(C):
        wp_scr[C * e : C * e + C, :] = w_ref[pl.ds(e, C, stride=C), :]


def grad_outer_kernel(g_ref, w_ref, goh_ref, gol_ref, wp_scr, wc_scr, r_scr):
    @pl.when(pl.program_id(0) == 0)
    def _():
        load_weight(w_ref, wp_scr)
        wh, wl = split(wp_scr[...])
        wc_scr[:, 0:Z] = wh
        wc_scr[:, Z : 2 * Z] = wl

    gh, gl = split(g_ref[...])
    r_scr[...] = dot(wc_scr[...], jnp.concatenate([gh, gh], axis=1), NT) + dot(wc_scr[:, 0:Z], gl, NT)
    for ip in range(2):
        for ep in range(16):
            x0 = r_scr[64 * ep : 64 * ep + 32, 128 * ip : 128 * ip + 128]
            x1 = r_scr[64 * ep + 32 : 64 * ep + 64, 128 * ip : 128 * ip + 128]
            for k, y in enumerate(half_swap(x0, x1)):
                hi, lo = split(y)
                row = (2 * ip + k) * C
                goh_ref[row : row + C, 128 * ep : 128 * ep + 128] = hi
                gol_ref[row : row + C, 128 * ep : 128 * ep + 128] = lo


def grad_right_kernel(l0_ref, l1_ref, l2_ref, l3_ref, goh_ref, gol_ref, own_ref, other_ref, a_scr, ac_scr, acc_scr, t_scr):
    n = pl.program_id(0)

    @pl.when(n == 0)
    def _():
        load_left((l0_ref, l1_ref, l2_ref, l3_ref), a_scr)
        ah, al = split(a_scr[...])
        ac_scr[0:S, :] = ah
        ac_scr[S : 2 * S, :] = al

    k = pl.ds(pl.multiple_of(n * 256, 256), 256)
    for q in range(4):
        cols = slice(512 * q, 512 * q + 512)
        r = dot(ac_scr[:, k], goh_ref[:, cols])
        r = r[:S] + r[S:] + dot(ac_scr[0:S, k], gol_ref[:, cols])

        @pl.when(n == 0)
        def _():
            acc_scr[:, cols] = r

        @pl.when(n == 1)
        def _():
            t_scr[cols, :] = ((acc_scr[:, cols] + r) * (1.0 / S)).T

    @pl.when(n == 1)
    def _():
        row = lax.axis_index("row") // 2
        y = lax.rem(row, 4)
        z = row // 4
        for m in range(16):
            block = jnp.concatenate([t_scr[pl.ds(4 * m + q, C, stride=TJ), :] for q in range(4)], axis=0)
            block = block.T
            for k in range(16):
                yy = lax.rem(k % 4 + 4 - y, 4)
                zz = lax.rem(k // 4 + 4 - z, 4)
                own_ref[yy, zz, :, 128 * m : 128 * m + 128] = block[4 * k : 4 * k + 4]
                other_ref[yy, zz, :, 128 * m : 128 * m + 128] = block[64 + 4 * k : 68 + 4 * k]


def outer_kernel(l0_ref, l1_ref, l2_ref, l3_ref, own_ref, other_ref, g_ref, oh_ref, ol_ref, bh_ref, bl_ref, gwo_ref, gwx_ref,
                 a_scr, at_scr, b_scr, t_scr, r_scr, gc_scr, w_scr):
    n = pl.program_id(0)

    @pl.when(n == 0)
    def _():
        load_left((l0_ref, l1_ref, l2_ref, l3_ref), a_scr)
        ath, atl = split(a_scr[...].T)
        at_scr[:, 0:S] = ath
        at_scr[:, S : 2 * S] = atl
        for k in range(16):
            b_scr[4 * k : 4 * k + 4, :] = own_ref[k]
            b_scr[64 + 4 * k : 68 + 4 * k, :] = other_ref[k]
        for m in range(16):
            t_scr[128 * m : 128 * m + 128, :] = b_scr[:, 128 * m : 128 * m + 128].T
        gh, gl = split(g_ref[...])
        gc_scr[:, 0:Z] = gh
        gc_scr[:, Z : 2 * Z] = gl

    for e in range(8):
        hi, lo = split(t_scr[pl.ds(8 * n + e, TJ, stride=C), :])
        bh_ref[TJ * e : TJ * e + TJ, :] = hi
        bl_ref[TJ * e : TJ * e + TJ, :] = lo
    for h in range(2):
        bh = bh_ref[256 * h : 256 * h + 256, :]
        bl = bl_ref[256 * h : 256 * h + 256, :]
        r_scr[h] = dot(at_scr[...], jnp.concatenate([bh, bh], axis=1), NT) + dot(at_scr[:, 0:S], bl, NT)
        for ep in range(2):
            for ip in range(8):
                x0 = r_scr[h, 64 * ip : 64 * ip + 32, 128 * ep : 128 * ep + 128]
                x1 = r_scr[h, 64 * ip + 32 : 64 * ip + 64, 128 * ep : 128 * ep + 128]
                for k, y in enumerate(half_swap(x0, x1)):
                    hi, lo = split(y)
                    row = (4 * h + 2 * ep + k) * C
                    oh_ref[row : row + C, 128 * ip : 128 * ip + 128] = hi
                    ol_ref[row : row + C, 128 * ip : 128 * ip + 128] = lo
    r = dot(oh_ref[...], gc_scr[...])
    rows = pl.ds(pl.multiple_of(n * 256, 256), 256)
    w_scr[rows, :] = (r[:, :Z] + r[:, Z:] + dot(ol_ref[...], gc_scr[:, 0:Z])) * (1.0 / S)

    @pl.when(n == 3)
    def _():
        core = core_index()
        bias = jnp.broadcast_to(jnp.sum(g_ref[...], axis=0, keepdims=True), (8, Z))
        for k in range(16):
            lo = w_scr[pl.ds(k, C, stride=C), :]
            hi = w_scr[pl.ds(16 + k, C, stride=C), :]
            gwo_ref[k, 0:C, :] = jnp.where(core == 0, lo, hi)
            gwx_ref[k, 0:C, :] = jnp.where(core == 0, hi, lo)
            gwo_ref[k, C : C + 8, :] = bias
            gwx_ref[k, C : C + 8, :] = bias


def pair_kernel(oh_ref, ol_ref, w_ref, b_ref, p_ref, wp_scr, wc_scr, acc_scr):
    n = pl.program_id(0)

    @pl.when(n == 0)
    def _():
        load_weight(w_ref, wp_scr)
        wth, wtl = split(wp_scr[...].T)
        wc_scr[0:Z, :] = wth
        wc_scr[Z : 2 * Z, :] = wtl

    k = pl.ds(pl.multiple_of(n * 256, 256), 256)
    for q in range(4):
        cols = slice(256 * q, 256 * q + 256)
        r = dot(wc_scr[:, k], oh_ref[:, cols])
        r = r[:Z] + r[Z:] + dot(wc_scr[0:Z, k], ol_ref[:, cols])

        @pl.when(n == 0)
        def _():
            acc_scr[:, cols] = r

        @pl.when((n > 0) & (n < 3))
        def _():
            acc_scr[:, cols] += r

        @pl.when(n == 3)
        def _():
            p_ref[cols, :] = ((acc_scr[:, cols] + r) * (1.0 / S)).T + b_ref[...]


def grad_left_kernel(goh_ref, gol_ref, bh_ref, bl_ref, gl_ref, s_scr):
    n = pl.program_id(0)

    bh = bh_ref[...]
    r = dot(goh_ref[...], jnp.concatenate([bh, bl_ref[...]], axis=1))
    r = (r[:, :S] + r[:, S:] + dot(gol_ref[...], bh)) * (1.0 / S)
    s_scr[:, pl.ds(pl.multiple_of(n * 256, 256), 256)] = r.T

    @pl.when(n == 1)
    def _():
        core = core_index()
        col = lax.axis_index("col")
        for q in range(8):
            own = s_scr[8 * q : 8 * q + 8, :]
            other = s_scr[64 + 8 * q : 72 + 8 * q, :]
            lo = jnp.where(core == 0, own, other)
            hi = jnp.where(core == 0, other, own)
            xx = lax.rem(q % 4 + 4 - lax.rem(col, 4), 4)
            zz = lax.rem(q // 4 + 2 - col // 4, 2)
            gl_ref[xx, zz, 0:8, :] = jnp.concatenate([lo[0:4], hi[0:4]], axis=0)
            gl_ref[xx, zz, 8:16, :] = jnp.concatenate([lo[4:8], hi[4:8]], axis=0)


def copies_kernel(x_ref, out_ref):
    for k in range(out_ref.shape[0]):
        out_ref[k] = x_ref[...]


def sum_spread_kernel(x_ref, out_ref):
    total = x_ref[0]
    for k in range(1, x_ref.shape[0]):
        total = total + x_ref[k]
    for k in range(out_ref.shape[0]):
        out_ref[k] = total


def sum_final_kernel(x_ref, out_ref, bias_ref):
    total = x_ref[0]
    for k in range(1, x_ref.shape[0]):
        total = total + x_ref[k]
    total = total * (1.0 / 512)
    for k in range(out_ref.shape[0]):
        out_ref[k] = total[:C]
    bias_ref[...] = total[C : C + 1]


def join_kernel(own_ref, other_ref, r0_ref, r1_ref, r2_ref, r3_ref, l0_ref, l1_ref, w_ref, gr_ref, gl_ref):
    core = core_index()
    for k in range(16):
        own = own_ref[k]
        other = other_ref[k]
        w_ref[C * k : C * k + C, :] = jnp.where(core == 0, own, other)
        w_ref[512 + C * k : 512 + C * k + C, :] = jnp.where(core == 0, other, own)
    gr_ref[...] = (r0_ref[0] + r1_ref[...]) + (r2_ref[...] + r3_ref[...])
    gl_ref[...] = l0_ref[0] + l1_ref[...]


def whole(shape):
    return pl.BlockSpec(shape, lambda n: (0,) * len(shape))


def rows_of(shape):
    return pl.BlockSpec(shape, lambda n: (n, 0))


def call(kernel, ins, outs, scratch, flops, nbytes, steps=4, limit=40):
    return pl.pallas_call(
        kernel,
        grid=(steps,),
        in_specs=ins,
        out_specs=[spec for _, _, spec in outs],
        out_shape=[pltpu.HBM(s, d) if d == BF16 else jax.ShapeDtypeStruct(s, d) for s, d, _ in outs],
        scratch_shapes=[pltpu.VMEM(s, d) for s, d in scratch],
        cost_estimate=pl.CostEstimate(flops=flops, bytes_accessed=nbytes, transcendentals=0),
        compiler_params=pltpu.CompilerParams(vmem_limit_bytes=limit << 20),
    )


LEFT = whole((2, 16, IC))
RIGHT = whole((16, 4, JE))
WHOLE_G = whole((IJ, Z))
WEIGHT = whole((CE, Z))
grad_outer_call = call(
    grad_outer_kernel,
    [rows_of((256, Z)), WEIGHT],
    [((IC, JE), BF16, rows_of((128, JE)))] * 2,
    [((CE, Z), F32), ((CE, 2 * Z), BF16), ((CE, 256), F32)],
    10**9, 5 << 20)
grad_right_call = call(
    grad_right_kernel,
    [LEFT, LEFT, LEFT, LEFT, rows_of((256, JE)), rows_of((256, JE))],
    [((4, 4, 4, JE), F32, whole((4, 4, 4, JE)))] * 2,
    [((S, IC), F32), ((2 * S, IC), BF16), ((S, JE), F32), ((JE, S), F32)],
    10**9, 5 << 20, 2)
outer_call = call(
    outer_kernel,
    [LEFT, LEFT, LEFT, LEFT, RIGHT, RIGHT, WHOLE_G],
    [((CE, IJ), BF16, rows_of((256, IJ)))] * 2 + [((JE, S), BF16, rows_of((512, S)))] * 2
    + [((16, 40, Z), F32, whole((16, 40, Z)))] * 2,
    [((S, IC), F32), ((IC, 2 * S), BF16), ((S, JE), F32), ((JE, S), F32), ((2, IC, 256), F32), ((IJ, 2 * Z), BF16), ((CE, Z), F32)],
    2 * 10**9, 7 << 20)
pair_call = call(
    pair_kernel,
    [rows_of((256, IJ))] * 2 + [WEIGHT, whole((1, Z))],
    [((IJ, Z), F32, whole((IJ, Z)))],
    [((CE, Z), F32), ((2 * Z, CE), BF16), ((Z, IJ), F32)],
    10**9, 5 << 20)
grad_left_call = call(
    grad_left_kernel,
    [rows_of((256, JE))] * 2 + [whole((JE, S))] * 2,
    [((4, 2, 16, IC), F32, whole((4, 2, 16, IC)))],
    [((S, IC), F32)],
    10**9, 6 << 20, 2)
join_call = call(
    join_kernel,
    [whole((16, C, Z))] * 2 + [whole((4, 4, JE))] + [whole((4, JE))] * 3 + [whole((2, 16, IC)), whole((16, IC))],
    [((CE, Z), F32, WEIGHT), ((4, JE), F32, whole((4, JE))), ((16, IC), F32, whole((16, IC)))],
    [], 10**5, 1 << 20, 1, 8)
copies_call = call(copies_kernel, [whole((4, JE))], [((16, 4, JE), F32, RIGHT)], [], 10**5, 1 << 19, 1, 8)
spread_call = call(sum_spread_kernel, [whole((16, 40, Z))], [((8, 40, Z), F32, whole((8, 40, Z)))], [], 10**5, 1 << 19, 1, 8)
final_call = call(
    sum_final_kernel,
    [whole((8, 40, Z))],
    [((16, C, Z), F32, whole((16, C, Z))), ((1, Z), F32, whole((1, Z)))],
    [], 10**5, 1 << 19, 1, 8)


def rid(z, y, c):
    return (z * 4 + y) * 2 + c


CORE = [(r, r ^ 1) for r in range(32)]
YZ = [[rid(z, y, c) for z in range(4) for y in range(4)] for c in range(2)]
XY = [[rid(z, y, c) * 8 + h * 4 + x for y in range(4) for x in range(4)] for z in range(4) for h in range(2) for c in range(2)]
Z8 = [[rid(z, y, c) * 8 + h * 4 + x for z in range(4) for h in range(2)] for y in range(4) for x in range(4) for c in range(2)]
BOTH = ("row", "col")
R4 = range(4)
Y_PERMS = [[(rid(z, y, c), rid(z, (y + k) % 4, c)) for z in R4 for y in R4 for c in range(2)] for k in (1, 2, 3)]
Z_PERMS = [[(rid(z, y, c), rid((z + k) % 4, y, c)) for z in R4 for y in R4 for c in range(2)] for k in (1, 2, 3)]
X_PERMS = [[(h * 4 + x, h * 4 + (x + k) % 4) for h in range(2) for x in R4] for k in (1, 2, 3)]
H_PERM = [(q, q ^ 4) for q in range(8)]


def in_hbm(*xs):
    return [pltpu.with_memory_space_constraint(x, pltpu.HBM) for x in xs]


def body(left, right, w_out, b_out, pair_grad):
    tie = lax.optimization_barrier
    g = pair_grad.reshape(IJ, Z)
    left_far = lax.ppermute(left, "col", H_PERM)
    (copies,) = copies_call(right)
    right_own = lax.all_to_all(copies, "row", 0, 0, axis_index_groups=YZ)
    left_pair = jnp.stack([left, left_far])
    pieces = [left_pair] + [lax.ppermute(left_pair, "col", p) for p in X_PERMS]
    goh, gol = grad_outer_call(*in_hbm(g, w_out))
    gr_own, gr_other = grad_right_call(*pieces, *in_hbm(goh, gol))
    right_other = lax.ppermute(right_own, "row", CORE)
    oh, ol, bh, bl, gw_own, gw_other = outer_call(*pieces, right_own, right_other, g)
    gw = gw_own + lax.ppermute(gw_other, "row", CORE)
    gw, goh, gol, bh, bl = tie((gw, goh, gol, bh, bl))
    gw = lax.all_to_all(gw, BOTH, 0, 0, axis_index_groups=XY)
    gr = gr_own + lax.ppermute(gr_other, "row", CORE)
    (gl,) = grad_left_call(*in_hbm(goh, gol, bh, bl))
    (gw,) = spread_call(gw)
    gw, oh, ol = tie((gw, oh, ol))
    gr = gr[0] + sum(lax.ppermute(gr[k + 1], "row", p) for k, p in enumerate(Y_PERMS))
    gl = gl[0] + sum(lax.ppermute(gl[k + 1], "col", p) for k, p in enumerate(X_PERMS))
    gw = lax.all_to_all(gw, BOTH, 0, 0, axis_index_groups=Z8)
    (pair_out,) = pair_call(*in_hbm(oh, ol, w_out), b_out.reshape(1, Z))
    gw, grad_bias = final_call(gw)
    gr_parts = [lax.ppermute(gr[k + 1], "row", p) for k, p in enumerate(Z_PERMS)]
    gl_part = lax.ppermute(gl[1], "col", H_PERM)
    gw_own = lax.all_to_all(gw, BOTH, 0, 0, axis_index_groups=XY)
    gw_other = lax.ppermute(gw_own, "row", CORE)
    grad_weight, grad_right, grad_left = join_call(gw_own, gw_other, gr, *gr_parts, gl, gl_part)
    return (pair_out.reshape(TI, TJ, Z), grad_left, grad_right, grad_weight, grad_bias.reshape(Z))


def solution(mesh):
    placed = (P("col", "row"), P("row", "col"), P(), P(), P("row", "col", None))
    return jax.shard_map(
        body,
        mesh=mesh,
        in_specs=placed,
        out_specs=(P("row", "col", None), P("col", "row"), P("row", "col"), P(), P()),
        check_vma=False,
    )
```

```python
import jax
import jax.numpy as jnp
from jax import lax
from jax.experimental import pallas as pl
from jax.experimental.pallas import tpu as pltpu
from jax.sharding import PartitionSpec as P


C = 32
Z = 128
S = 128
TI = 16
TJ = 64
IC = TI * C
JE = TJ * C
IJ = TI * TJ
CE = C * C
F32 = jnp.float32
BF16 = jnp.bfloat16
NT = (((1,), (1,)), ((), ()))
NN = (((1,), (0,)), ((), ()))


def split(x):
    hi = x.astype(BF16)
    return hi, (x - hi.astype(F32)).astype(BF16)


def dot(x, y, dims=NN):
    return lax.dot_general(x, y, dims, preferred_element_type=F32)


def half_swap(x0, x1):
    lane = lax.broadcasted_iota(jnp.int32, x0.shape, 1)
    low = lane < 64
    r0 = pltpu.roll(x0, 64, 1)
    r1 = pltpu.roll(x1, 64, 1)
    return jnp.where(low, x0, r1), jnp.where(low, r0, x1)


def core_index():
    return lax.rem(lax.axis_index("row"), 2)


def load_left(piece_refs, a_scr):
    core = core_index()
    col = lax.axis_index("col")
    for p, ref in enumerate(piece_refs):
        for h, half in ((0, col // 4), (1, 1 - col // 4)):
            q = half * 4 + lax.rem(col + 4 - p, 4)
            x = ref[h]
            lo = jnp.concatenate([x[0:4], x[8:12]], axis=0)
            hi = jnp.concatenate([x[4:8], x[12:16]], axis=0)
            a_scr[pl.ds(pl.multiple_of(q * 8, 8), 8), :] = jnp.where(core == 0, lo, hi)
            a_scr[pl.ds(pl.multiple_of(64 + q * 8, 8), 8), :] = jnp.where(core == 0, hi, lo)


def load_weight(w_ref, wp_scr):
    for e in range(C):
        wp_scr[C * e : C * e + C, :] = w_ref[pl.ds(e, C, stride=C), :]


def slot_of(k):
    return jnp.where(k == 0, 0, jnp.where(k == 3, 1, k + 1))


def grads_kernel(l0_ref, l1_ref, l2_ref, l3_ref, g_hbm, w_hbm, goh_hbm, gol_hbm, own_ref, other_ref,
                 a_scr, ac_scr, g_scr, w_scr, wp_scr, wc_scr, r_scr, goh_scr, gol_scr, t_scr, in_sem, out_sem):
    get_w = pltpu.make_async_copy(w_hbm, w_scr, in_sem.at[0])
    get_g = pltpu.make_async_copy(g_hbm, g_scr, in_sem.at[1])
    get_w.start()
    get_g.start()
    load_left((l0_ref, l1_ref, l2_ref, l3_ref), a_scr)
    ah, al = split(a_scr[...])
    ac_scr[0:S, :] = ah
    ac_scr[S : 2 * S, :] = al
    get_w.wait()
    load_weight(w_scr, wp_scr)
    wh, wl = split(wp_scr[...])
    wc_scr[:, 0:Z] = wh
    wc_scr[:, Z : 2 * Z] = wl
    get_g.wait()

    def puts(n):
        rows = pl.ds(pl.multiple_of(n * 128, 128), 128)
        return (
            pltpu.make_async_copy(goh_scr.at[rows, :], goh_hbm.at[rows, :], out_sem.at[0, n]),
            pltpu.make_async_copy(gol_scr.at[rows, :], gol_hbm.at[rows, :], out_sem.at[1, n]),
        )

    @pl.loop(0, 4)
    def _(n):
        gh, gl = split(g_scr[pl.ds(pl.multiple_of(n * 256, 256), 256), :])
        r_scr[...] = dot(wc_scr[...], jnp.concatenate([gh, gh], axis=1), NT) + dot(wc_scr[:, 0:Z], gl, NT)
        for ip in range(2):
            for ep in range(16):
                x0 = r_scr[64 * ep : 64 * ep + 32, 128 * ip : 128 * ip + 128]
                x1 = r_scr[64 * ep + 32 : 64 * ep + 64, 128 * ip : 128 * ip + 128]
                for k, y in enumerate(half_swap(x0, x1)):
                    hi, lo = split(y)
                    rows = pl.ds(pl.multiple_of((4 * n + 2 * ip + k) * C, C), C)
                    goh_scr[rows, 128 * ep : 128 * ep + 128] = hi
                    gol_scr[rows, 128 * ep : 128 * ep + 128] = lo
        for put in puts(n):
            put.start()

    @pl.loop(0, 8)
    def _(n):
        cols = pl.ds(pl.multiple_of(n * 256, 256), 256)
        r = dot(ac_scr[...], goh_scr[:, cols])
        r = r[:S] + r[S:] + dot(ac_scr[0:S, :], gol_scr[:, cols])
        t_scr[cols, :] = (r * (1.0 / S)).T

    row = lax.axis_index("row") // 2
    y = lax.rem(row, 4)
    z = row // 4
    for m in range(16):
        block = jnp.concatenate([t_scr[pl.ds(4 * m + q, C, stride=TJ), :] for q in range(4)], axis=0)
        block = block.T
        for k in range(16):
            yy = slot_of((k % 4) ^ y)
            zz = slot_of((k // 4) ^ z)
            own_ref[yy, zz, :, 128 * m : 128 * m + 128] = block[4 * k : 4 * k + 4]
            other_ref[yy, zz, :, 128 * m : 128 * m + 128] = block[64 + 4 * k : 68 + 4 * k]
    for n in range(4):
        for put in puts(n):
            put.wait()


def outer_kernel(l0_ref, l1_ref, l2_ref, l3_ref, own_ref, other_ref, g_ref, oh_ref, ol_ref, bh_ref, bl_ref, gwo_ref, gwx_ref,
                 a_scr, at_scr, b_scr, t_scr, r_scr, gc_scr, w_scr):
    n = pl.program_id(0)

    @pl.when(n == 0)
    def _():
        load_left((l0_ref, l1_ref, l2_ref, l3_ref), a_scr)
        ath, atl = split(a_scr[...].T)
        at_scr[:, 0:S] = ath
        at_scr[:, S : 2 * S] = atl
        for k in range(16):
            b_scr[4 * k : 4 * k + 4, :] = own_ref[k]
            b_scr[64 + 4 * k : 68 + 4 * k, :] = other_ref[k]
        for m in range(16):
            t_scr[128 * m : 128 * m + 128, :] = b_scr[:, 128 * m : 128 * m + 128].T
        gh, gl = split(g_ref[...])
        gc_scr[:, 0:Z] = gh
        gc_scr[:, Z : 2 * Z] = gl

    for e in range(8):
        hi, lo = split(t_scr[pl.ds(8 * n + e, TJ, stride=C), :])
        bh_ref[TJ * e : TJ * e + TJ, :] = hi
        bl_ref[TJ * e : TJ * e + TJ, :] = lo
    for h in range(2):
        bh = bh_ref[256 * h : 256 * h + 256, :]
        bl = bl_ref[256 * h : 256 * h + 256, :]
        r_scr[h] = dot(at_scr[...], jnp.concatenate([bh, bh], axis=1), NT) + dot(at_scr[:, 0:S], bl, NT)
        for ep in range(2):
            for ip in range(8):
                x0 = r_scr[h, 64 * ip : 64 * ip + 32, 128 * ep : 128 * ep + 128]
                x1 = r_scr[h, 64 * ip + 32 : 64 * ip + 64, 128 * ep : 128 * ep + 128]
                for k, y in enumerate(half_swap(x0, x1)):
                    hi, lo = split(y)
                    row = (4 * h + 2 * ep + k) * C
                    oh_ref[row : row + C, 128 * ip : 128 * ip + 128] = hi
                    ol_ref[row : row + C, 128 * ip : 128 * ip + 128] = lo
    r = dot(oh_ref[...], gc_scr[...])
    rows = pl.ds(pl.multiple_of(n * 256, 256), 256)
    w_scr[rows, :] = (r[:, :Z] + r[:, Z:] + dot(ol_ref[...], gc_scr[:, 0:Z])) * (1.0 / S)

    @pl.when(n == 3)
    def _():
        core = core_index()
        bias = jnp.broadcast_to(jnp.sum(g_ref[...], axis=0, keepdims=True), (8, Z))
        for k in range(16):
            lo = w_scr[pl.ds(k, C, stride=C), :]
            hi = w_scr[pl.ds(16 + k, C, stride=C), :]
            gwo_ref[k, 0:C, :] = jnp.where(core == 0, lo, hi)
            gwx_ref[k, 0:C, :] = jnp.where(core == 0, hi, lo)
            gwo_ref[k, C : C + 8, :] = bias
            gwx_ref[k, C : C + 8, :] = bias


def pair_kernel(oh_hbm, ol_hbm, w_hbm, b_ref, p_hbm, oh_scr, ol_scr, w_scr, wp_scr, wc_scr, p_scr, in_sem, out_sem):
    get_w = pltpu.make_async_copy(w_hbm, w_scr, in_sem.at[0])
    get_h = pltpu.make_async_copy(oh_hbm, oh_scr, in_sem.at[1])
    get_l = pltpu.make_async_copy(ol_hbm, ol_scr, in_sem.at[2])
    get_w.start()
    get_h.start()
    get_l.start()
    get_w.wait()
    load_weight(w_scr, wp_scr)
    wth, wtl = split(wp_scr[...].T)
    wc_scr[0:Z, :] = wth
    wc_scr[Z : 2 * Z, :] = wtl
    get_h.wait()
    get_l.wait()

    def put(n):
        rows = pl.ds(pl.multiple_of(n * 256, 256), 256)
        return pltpu.make_async_copy(p_scr.at[rows, :], p_hbm.at[rows, :], out_sem.at[n])

    @pl.loop(0, 4)
    def _(n):
        cols = pl.ds(pl.multiple_of(n * 256, 256), 256)
        r = dot(wc_scr[...], oh_scr[:, cols])
        r = r[:Z] + r[Z:] + dot(wc_scr[0:Z, :], ol_scr[:, cols])
        p_scr[cols, :] = (r * (1.0 / S)).T + b_ref[...]
        put(n).start()

    for n in range(4):
        put(n).wait()


def grad_left_kernel(goh_ref, gol_ref, bh_ref, bl_ref, gl_ref, s_scr):
    n = pl.program_id(0)

    bh = bh_ref[...]
    r = dot(goh_ref[...], jnp.concatenate([bh, bl_ref[...]], axis=1))
    r = (r[:, :S] + r[:, S:] + dot(gol_ref[...], bh)) * (1.0 / S)
    s_scr[:, pl.ds(pl.multiple_of(n * 256, 256), 256)] = r.T

    @pl.when(n == 1)
    def _():
        core = core_index()
        col = lax.axis_index("col")
        for q in range(8):
            own = s_scr[8 * q : 8 * q + 8, :]
            other = s_scr[64 + 8 * q : 72 + 8 * q, :]
            lo = jnp.where(core == 0, own, other)
            hi = jnp.where(core == 0, other, own)
            xx = slot_of((q % 4) ^ lax.rem(col, 4))
            zz = lax.rem(q // 4 + 2 - col // 4, 2)
            gl_ref[xx, zz, 0:8, :] = jnp.concatenate([lo[0:4], hi[0:4]], axis=0)
            gl_ref[xx, zz, 8:16, :] = jnp.concatenate([lo[4:8], hi[4:8]], axis=0)


def copies_kernel(x_ref, out_ref):
    for k in range(out_ref.shape[0]):
        out_ref[k] = x_ref[...]


def sum_spread_kernel(x_ref, out_ref):
    total = x_ref[0]
    for k in range(1, x_ref.shape[0]):
        total = total + x_ref[k]
    for k in range(out_ref.shape[0]):
        out_ref[k] = total


def sum_final_kernel(x_ref, out_ref, bias_ref):
    total = x_ref[0]
    for k in range(1, x_ref.shape[0]):
        total = total + x_ref[k]
    total = total * (1.0 / 512)
    for k in range(out_ref.shape[0]):
        out_ref[k] = total[:C]
    bias_ref[...] = total[C : C + 1]


def join_kernel(own_ref, other_ref, r0_ref, r1_ref, l0_ref, l1_ref, w_ref, gr_ref, gl_ref):
    core = core_index()
    for k in range(16):
        own = own_ref[k]
        other = other_ref[k]
        w_ref[C * k : C * k + C, :] = jnp.where(core == 0, own, other)
        w_ref[512 + C * k : 512 + C * k + C, :] = jnp.where(core == 0, other, own)
    gr_ref[...] = r0_ref[0] + r1_ref[...]
    gl_ref[...] = l0_ref[0] + l1_ref[...]


def whole(shape):
    return pl.BlockSpec(shape, lambda n: (0,) * len(shape))


def rows_of(shape):
    return pl.BlockSpec(shape, lambda n: (n, 0))


def call(kernel, ins, outs, scratch, flops, nbytes, steps=4, limit=40):
    return pl.pallas_call(
        kernel,
        grid=(steps,),
        in_specs=ins,
        out_specs=[spec for _, _, spec in outs],
        out_shape=[pltpu.HBM(s, d) if d == BF16 else jax.ShapeDtypeStruct(s, d) for s, d, _ in outs],
        scratch_shapes=[pltpu.VMEM(s, d) for s, d in scratch],
        cost_estimate=pl.CostEstimate(flops=flops, bytes_accessed=nbytes, transcendentals=0),
        compiler_params=pltpu.CompilerParams(vmem_limit_bytes=limit << 20),
    )


LEFT = whole((2, 16, IC))
RIGHT = whole((16, 4, JE))
WHOLE_G = whole((IJ, Z))
WEIGHT = whole((CE, Z))
ANY = pl.BlockSpec(memory_space=pl.ANY)
VM = pl.BlockSpec(memory_space=pltpu.VMEM)
DMA = pltpu.SemaphoreType.DMA


def flat_call(kernel, ins, outs, scratch, sems, flops, nbytes):
    return pl.pallas_call(
        kernel,
        in_specs=ins,
        out_specs=[spec for _, spec in outs],
        out_shape=[shape for shape, _ in outs],
        scratch_shapes=[pltpu.VMEM(s, d) for s, d in scratch] + [DMA(s) for s in sems],
        cost_estimate=pl.CostEstimate(flops=flops, bytes_accessed=nbytes, transcendentals=0),
        compiler_params=pltpu.CompilerParams(vmem_limit_bytes=40 << 20),
    )


GR_PART = (jax.ShapeDtypeStruct((4, 4, 4, JE), F32), VM)
grads_call = flat_call(
    grads_kernel,
    [VM] * 4 + [ANY] * 2,
    [(pltpu.HBM((IC, JE), BF16), ANY)] * 2 + [GR_PART] * 2,
    [((S, IC), F32), ((2 * S, IC), BF16), ((IJ, Z), F32), ((CE, Z), F32), ((CE, Z), F32), ((CE, 2 * Z), BF16),
     ((CE, 256), F32), ((IC, JE), BF16), ((IC, JE), BF16), ((JE, S), F32)],
    [(2,), (2, 4)],
    2 * 10**9, 6 << 20)
outer_call = call(
    outer_kernel,
    [LEFT, LEFT, LEFT, LEFT, RIGHT, RIGHT, WHOLE_G],
    [((CE, IJ), BF16, rows_of((256, IJ)))] * 2 + [((JE, S), BF16, rows_of((512, S)))] * 2
    + [((16, 40, Z), F32, whole((16, 40, Z)))] * 2,
    [((S, IC), F32), ((IC, 2 * S), BF16), ((S, JE), F32), ((JE, S), F32), ((2, IC, 256), F32), ((IJ, 2 * Z), BF16), ((CE, Z), F32)],
    2 * 10**9, 7 << 20)
pair_call = flat_call(
    pair_kernel,
    [ANY] * 3 + [VM],
    [(pltpu.HBM((IJ, Z), F32), ANY)],
    [((CE, IJ), BF16), ((CE, IJ), BF16), ((CE, Z), F32), ((CE, Z), F32), ((2 * Z, CE), BF16), ((IJ, Z), F32)],
    [(3,), (4,)],
    10**9, 5 << 20)
grad_left_call = call(
    grad_left_kernel,
    [rows_of((256, JE))] * 2 + [whole((JE, S))] * 2,
    [((4, 2, 16, IC), F32, whole((4, 2, 16, IC)))],
    [((S, IC), F32)],
    10**9, 6 << 20, 2)
join_call = call(
    join_kernel,
    [whole((16, C, Z))] * 2 + [whole((2, 4, JE)), whole((4, JE)), whole((2, 16, IC)), whole((16, IC))],
    [((CE, Z), F32, WEIGHT), ((4, JE), F32, whole((4, JE))), ((16, IC), F32, whole((16, IC)))],
    [], 10**5, 1 << 20, 1, 8)
copies_call = call(copies_kernel, [whole((4, JE))], [((16, 4, JE), F32, RIGHT)], [], 10**5, 1 << 19, 1, 8)
spread_call = call(sum_spread_kernel, [whole((16, 40, Z))], [((8, 40, Z), F32, whole((8, 40, Z)))], [], 10**5, 1 << 19, 1, 8)
final_call = call(
    sum_final_kernel,
    [whole((8, 40, Z))],
    [((16, C, Z), F32, whole((16, C, Z))), ((1, Z), F32, whole((1, Z)))],
    [], 10**5, 1 << 19, 1, 8)


def rid(z, y, c):
    return (z * 4 + y) * 2 + c


CORE = [(r, r ^ 1) for r in range(32)]
YZ = [[rid(z, y, c) for z in range(4) for y in range(4)] for c in range(2)]
XY = [[rid(z, y, c) * 8 + h * 4 + x for y in range(4) for x in range(4)] for z in range(4) for h in range(2) for c in range(2)]
Z8 = [[rid(z, y, c) * 8 + h * 4 + x for z in range(4) for h in range(2)] for y in range(4) for x in range(4) for c in range(2)]
BOTH = ("row", "col")
R4 = range(4)
Y_FLIP = {k: [(rid(z, y, c), rid(z, y ^ k, c)) for z in R4 for y in R4 for c in range(2)] for k in (1, 3)}
Z_FLIP = {k: [(rid(z, y, c), rid(z ^ k, y, c)) for z in R4 for y in R4 for c in range(2)] for k in (1, 3)}
X_FLIP = {k: [(q, q ^ k) for q in range(8)] for k in (1, 3)}
X_PERMS = [[(h * 4 + x, h * 4 + (x + k) % 4) for h in range(2) for x in R4] for k in (1, 2, 3)]
H_PERM = [(q, q ^ 4) for q in range(8)]


def in_hbm(*xs):
    return [pltpu.with_memory_space_constraint(x, pltpu.HBM) for x in xs]


def body(left, right, w_out, b_out, pair_grad):
    tie = lax.optimization_barrier
    g = pair_grad.reshape(IJ, Z)
    left_far = lax.ppermute(left, "col", H_PERM)
    (copies,) = copies_call(*in_hbm(right))
    right_own = lax.all_to_all(copies, "row", 0, 0, axis_index_groups=YZ)
    left_pair = jnp.stack([left, left_far])
    pieces = [left_pair] + [lax.ppermute(left_pair, "col", p) for p in X_PERMS]
    goh, gol, gr_own, gr_other = grads_call(*pieces, *in_hbm(g, w_out))
    right_other = lax.ppermute(right_own, "row", CORE)
    oh, ol, bh, bl, gw_own, gw_other = outer_call(*pieces, right_own, right_other, g)
    gw = gw_own + lax.ppermute(gw_other, "row", CORE)
    gw, goh, gol, bh, bl = tie((gw, goh, gol, bh, bl))
    gw = lax.all_to_all(gw, BOTH, 0, 0, axis_index_groups=XY)
    gr = gr_own + lax.ppermute(gr_other, "row", CORE)
    (gl,) = grad_left_call(*in_hbm(goh, gol, bh, bl))
    (gw,) = spread_call(gw)
    gw, oh, ol = tie((gw, oh, ol))
    gr = gr[:2] + lax.ppermute(gr[2:], "row", Y_FLIP[1])
    gr = gr[0] + lax.ppermute(gr[1], "row", Y_FLIP[3])
    gl = gl[:2] + lax.ppermute(gl[2:], "col", X_FLIP[1])
    gl = gl[0] + lax.ppermute(gl[1], "col", X_FLIP[3])
    gw = lax.all_to_all(gw, BOTH, 0, 0, axis_index_groups=Z8)
    (pair_out,) = pair_call(*in_hbm(oh, ol, w_out), b_out.reshape(1, Z))
    gw, grad_bias = final_call(gw)
    gr = gr[:2] + lax.ppermute(gr[2:], "row", Z_FLIP[1])
    gr_part = lax.ppermute(gr[1], "row", Z_FLIP[3])
    gl_part = lax.ppermute(gl[1], "col", H_PERM)
    gw_own = lax.all_to_all(gw, BOTH, 0, 0, axis_index_groups=XY)
    gw_other = lax.ppermute(gw_own, "row", CORE)
    grad_weight, grad_right, grad_left = join_call(gw_own, gw_other, gr, gr_part, gl, gl_part)
    return (pair_out.reshape(TI, TJ, Z), grad_left, grad_right, grad_weight, grad_bias.reshape(Z))


def solution(mesh):
    placed = (P("col", "row"), P("row", "col"), P(), P(), P("row", "col", None))
    return jax.shard_map(
        body,
        mesh=mesh,
        in_specs=placed,
        out_specs=(P("row", "col", None), P("col", "row"), P("row", "col"), P(), P()),
        check_vma=False,
    )
```

```python
import jax
import jax.numpy as jnp
from jax import lax
from jax.experimental import pallas as pl
from jax.experimental.pallas import tpu as pltpu
from jax.sharding import PartitionSpec as P


C = 32
Z = 128
S = 128
TI = 16
TJ = 64
IC = TI * C
JE = TJ * C
IJ = TI * TJ
CE = C * C
F32 = jnp.float32
BF16 = jnp.bfloat16
NT = (((1,), (1,)), ((), ()))
NN = (((1,), (0,)), ((), ()))


def split(x):
    hi = x.astype(BF16)
    return hi, (x - hi.astype(F32)).astype(BF16)


def dot(x, y, dims=NN):
    return lax.dot_general(x, y, dims, preferred_element_type=F32)


def half_swap(x0, x1):
    lane = lax.broadcasted_iota(jnp.int32, x0.shape, 1)
    low = lane < 64
    r0 = pltpu.roll(x0, 64, 1)
    r1 = pltpu.roll(x1, 64, 1)
    return jnp.where(low, x0, r1), jnp.where(low, r0, x1)


def core_index():
    return lax.rem(lax.axis_index("row"), 2)


def load_left(piece_refs, a_scr):
    core = core_index()
    col = lax.axis_index("col")
    for p, ref in enumerate(piece_refs):
        for h, half in ((0, col // 4), (1, 1 - col // 4)):
            q = half * 4 + lax.rem(col + 4 - p, 4)
            x = ref[h]
            lo = jnp.concatenate([x[0:4], x[8:12]], axis=0)
            hi = jnp.concatenate([x[4:8], x[12:16]], axis=0)
            a_scr[pl.ds(pl.multiple_of(q * 8, 8), 8), :] = jnp.where(core == 0, lo, hi)
            a_scr[pl.ds(pl.multiple_of(64 + q * 8, 8), 8), :] = jnp.where(core == 0, hi, lo)


def load_weight(w_ref, wp_scr):
    for e in range(C):
        wp_scr[C * e : C * e + C, :] = w_ref[pl.ds(e, C, stride=C), :]


def slot_of(k):
    return jnp.where(k == 0, 0, jnp.where(k == 3, 1, k + 1))


def grads_kernel(l0_ref, l1_ref, l2_ref, l3_ref, g_hbm, w_hbm, goh_hbm, gol_hbm, own_ref, other_ref,
                 at_ref, gc_ref, bias_ref, a_scr, ac_scr, g_scr, w_scr, wp_scr, wc_scr, r_scr, goh_scr, gol_scr, t_scr, in_sem, out_sem):
    get_w = pltpu.make_async_copy(w_hbm, w_scr, in_sem.at[0])
    get_g = pltpu.make_async_copy(g_hbm, g_scr, in_sem.at[1])
    get_w.start()
    get_g.start()
    load_left((l0_ref, l1_ref, l2_ref, l3_ref), a_scr)
    ah, al = split(a_scr[...])
    ac_scr[0:S, :] = ah
    ac_scr[S : 2 * S, :] = al
    ath, atl = split(a_scr[...].T)
    at_ref[:, 0:S] = ath
    at_ref[:, S : 2 * S] = atl
    at_ref[:, 2 * S : 3 * S] = ath
    get_w.wait()
    load_weight(w_scr, wp_scr)
    wh, wl = split(wp_scr[...])
    wc_scr[:, 0:Z] = wh
    wc_scr[:, Z : 2 * Z] = wl
    wc_scr[:, 2 * Z : 3 * Z] = wh
    get_g.wait()
    bias_ref[...] = jnp.broadcast_to(jnp.sum(g_scr[...], axis=0, keepdims=True), (8, Z))

    def puts(n):
        rows = pl.ds(pl.multiple_of(n * 128, 128), 128)
        return (
            pltpu.make_async_copy(goh_scr.at[rows, :], goh_hbm.at[rows, :], out_sem.at[0, n]),
            pltpu.make_async_copy(gol_scr.at[rows, :], gol_hbm.at[rows, :], out_sem.at[1, n]),
        )

    @pl.loop(0, 4)
    def _(n):
        part = pl.ds(pl.multiple_of(n * 256, 256), 256)
        gh, gl = split(g_scr[part, :])
        gc_ref[part, 0:Z] = gh
        gc_ref[part, Z : 2 * Z] = gl
        r_scr[...] = dot(wc_scr[...], jnp.concatenate([gh, gh, gl], axis=1), NT)
        for ip in range(2):
            for ep in range(16):
                x0 = r_scr[64 * ep : 64 * ep + 32, 128 * ip : 128 * ip + 128]
                x1 = r_scr[64 * ep + 32 : 64 * ep + 64, 128 * ip : 128 * ip + 128]
                for k, y in enumerate(half_swap(x0, x1)):
                    hi, lo = split(y)
                    rows = pl.ds(pl.multiple_of((4 * n + 2 * ip + k) * C, C), C)
                    goh_scr[rows, 128 * ep : 128 * ep + 128] = hi
                    gol_scr[rows, 128 * ep : 128 * ep + 128] = lo
        for put in puts(n):
            put.start()

    @pl.loop(0, 8)
    def _(n):
        cols = pl.ds(pl.multiple_of(n * 256, 256), 256)
        r = dot(ac_scr[...], goh_scr[:, cols])
        r = r[:S] + r[S:] + dot(ac_scr[0:S, :], gol_scr[:, cols])
        t_scr[cols, :] = (r * (1.0 / S)).T

    row = lax.axis_index("row") // 2
    y = lax.rem(row, 4)
    z = row // 4
    for m in range(16):
        block = jnp.concatenate([t_scr[pl.ds(4 * m + q, C, stride=TJ), :] for q in range(4)], axis=0)
        block = block.T
        for k in range(16):
            yy = slot_of((k % 4) ^ y)
            zz = slot_of((k // 4) ^ z)
            own_ref[yy, zz, :, 128 * m : 128 * m + 128] = block[4 * k : 4 * k + 4]
            other_ref[yy, zz, :, 128 * m : 128 * m + 128] = block[64 + 4 * k : 68 + 4 * k]
    for n in range(4):
        for put in puts(n):
            put.wait()


def outer_kernel(at_ref, gc_ref, bias_ref, own_ref, other_ref, oh_hbm, ol_hbm, bc_hbm, gwo_ref, gwx_ref,
                 b_scr, t_scr, bc_scr, r0_scr, r1_scr, oh_scr, ol_scr, w_scr, b_sem, o_sem):
    for k in range(16):
        b_scr[4 * k : 4 * k + 4, :] = own_ref[k]
        b_scr[64 + 4 * k : 68 + 4 * k, :] = other_ref[k]
    for m in range(16):
        t_scr[128 * m : 128 * m + 128, :] = b_scr[:, 128 * m : 128 * m + 128].T
    for e in range(C):
        hi, lo = split(t_scr[pl.ds(e, TJ, stride=C), :])
        rows = slice(TJ * e, TJ * e + TJ)
        bc_scr[rows, 0:S] = hi
        bc_scr[rows, S : 2 * S] = hi
        bc_scr[rows, 2 * S : 3 * S] = lo
    puts = [pltpu.make_async_copy(bc_scr.at[:, S : 3 * S], bc_hbm, b_sem.at[0])]
    puts[0].start()
    r_scr = (r0_scr, r1_scr)

    def multiply(n):
        r_scr[n % 2][...] = dot(at_ref[...], bc_scr[256 * n : 256 * n + 256, :], NT)

    def weigh(m):
        rows = slice(256 * m, 256 * m + 256)
        hi = jnp.concatenate([oh_scr[q, rows, :] for q in range(4)], axis=1)
        lo = jnp.concatenate([ol_scr[q, rows, :] for q in range(4)], axis=1)
        r = dot(hi, gc_ref[...])
        w_scr[rows, :] = (r[:, :Z] + r[:, Z:] + dot(lo, gc_ref[:, 0:Z])) * (1.0 / S)

    multiply(0)
    for n in range(8):
        if n < 7:
            multiply(n + 1)
        if n in (2, 4, 6):
            weigh(n // 2 - 1)
        for ep in range(2):
            for ip in range(8):
                x0 = r_scr[n % 2][64 * ip : 64 * ip + 32, 128 * ep : 128 * ep + 128]
                x1 = r_scr[n % 2][64 * ip + 32 : 64 * ip + 64, 128 * ep : 128 * ep + 128]
                for k, y in enumerate(half_swap(x0, x1)):
                    hi, lo = split(y)
                    row = (4 * n + 2 * ep + k) * C
                    cols = slice(128 * (ip % 2), 128 * (ip % 2) + 128)
                    oh_scr[ip // 2, row : row + C, cols] = hi
                    ol_scr[ip // 2, row : row + C, cols] = lo
        if n % 2 == 1:
            rows = slice(128 * (n - 1), 128 * (n + 1))
            for i, (src, dst) in enumerate(((oh_scr, oh_hbm), (ol_scr, ol_hbm))):
                put = pltpu.make_async_copy(src.at[:, rows, :], dst.at[:, rows, :], o_sem.at[i, n // 2])
                put.start()
                puts.append(put)
    weigh(3)
    core = core_index()
    for k in range(16):
        lo = w_scr[pl.ds(k, C, stride=C), :]
        hi = w_scr[pl.ds(16 + k, C, stride=C), :]
        gwo_ref[k, 0:C, :] = jnp.where(core == 0, lo, hi)
        gwx_ref[k, 0:C, :] = jnp.where(core == 0, hi, lo)
        gwo_ref[k, C : C + 8, :] = bias_ref[...]
        gwx_ref[k, C : C + 8, :] = bias_ref[...]
    for put in puts:
        put.wait()


def pair_kernel(oh_hbm, ol_hbm, w_hbm, b_ref, p_hbm, oh_scr, ol_scr, w_scr, wp_scr, wc_scr, p_scr, w_sem, in_sem, out_sem):
    get_w = pltpu.make_async_copy(w_hbm, w_scr, w_sem.at[0])
    get_w.start()

    def gets(n):
        return (
            pltpu.make_async_copy(oh_hbm.at[n], oh_scr.at[n], in_sem.at[0, n]),
            pltpu.make_async_copy(ol_hbm.at[n], ol_scr.at[n], in_sem.at[1, n]),
        )

    for n in range(4):
        for get in gets(n):
            get.start()
    get_w.wait()
    load_weight(w_scr, wp_scr)
    wth, wtl = split(wp_scr[...].T)
    wc_scr[0:Z, :] = wth
    wc_scr[Z : 2 * Z, :] = wtl

    def put(n):
        rows = pl.ds(pl.multiple_of(n * 256, 256), 256)
        return pltpu.make_async_copy(p_scr.at[rows, :], p_hbm.at[rows, :], out_sem.at[n])

    @pl.loop(0, 4)
    def _(n):
        for get in gets(n):
            get.wait()
        r = dot(wc_scr[...], oh_scr[n])
        r = r[:Z] + r[Z:] + dot(wc_scr[0:Z, :], ol_scr[n])
        p_scr[pl.ds(pl.multiple_of(n * 256, 256), 256), :] = (r * (1.0 / S)).T + b_ref[...]
        put(n).start()

    for n in range(4):
        put(n).wait()


def grad_left_kernel(goh_hbm, gol_hbm, bc_hbm, gl_ref, goh_scr, gol_scr, bc_scr, s_scr, b_sem, in_sem):
    get_b = pltpu.make_async_copy(bc_hbm, bc_scr, b_sem.at[0])
    get_b.start()
    gets = []
    for n in range(4):
        rows = slice(128 * n, 128 * n + 128)
        for i, (src, dst) in enumerate(((goh_hbm, goh_scr), (gol_hbm, gol_scr))):
            get = pltpu.make_async_copy(src.at[rows, :], dst.at[rows, :], in_sem.at[i, n])
            get.start()
            gets.append(get)
    get_b.wait()
    for n in range(2):
        for get in gets[4 * n : 4 * n + 4]:
            get.wait()
        rows = slice(256 * n, 256 * n + 256)
        r = dot(goh_scr[rows, :], bc_scr[...])
        r = (r[:, :S] + r[:, S:] + dot(gol_scr[rows, :], bc_scr[:, 0:S])) * (1.0 / S)
        s_scr[:, rows] = r.T
    core = core_index()
    col = lax.axis_index("col")
    for q in range(8):
        own = s_scr[8 * q : 8 * q + 8, :]
        other = s_scr[64 + 8 * q : 72 + 8 * q, :]
        lo = jnp.where(core == 0, own, other)
        hi = jnp.where(core == 0, other, own)
        xx = slot_of((q % 4) ^ lax.rem(col, 4))
        zz = lax.rem(q // 4 + 2 - col // 4, 2)
        gl_ref[xx, zz, 0:8, :] = jnp.concatenate([lo[0:4], hi[0:4]], axis=0)
        gl_ref[xx, zz, 8:16, :] = jnp.concatenate([lo[4:8], hi[4:8]], axis=0)


def copies_kernel(x_ref, out_ref):
    for k in range(out_ref.shape[0]):
        out_ref[k] = x_ref[...]


def sum_spread_kernel(x_ref, out_ref):
    total = x_ref[0]
    for k in range(1, x_ref.shape[0]):
        total = total + x_ref[k]
    for k in range(out_ref.shape[0]):
        out_ref[k] = total


def sum_final_kernel(x_ref, out_ref, bias_ref):
    total = x_ref[0]
    for k in range(1, x_ref.shape[0]):
        total = total + x_ref[k]
    total = total * (1.0 / 512)
    for k in range(out_ref.shape[0]):
        out_ref[k] = total[:C]
    bias_ref[...] = total[C : C + 1]


def join_kernel(own_ref, other_ref, r0_ref, r1_ref, l0_ref, l1_ref, w_ref, gr_ref, gl_ref):
    core = core_index()
    for k in range(16):
        own = own_ref[k]
        other = other_ref[k]
        w_ref[C * k : C * k + C, :] = jnp.where(core == 0, own, other)
        w_ref[512 + C * k : 512 + C * k + C, :] = jnp.where(core == 0, other, own)
    gr_ref[...] = r0_ref[0] + r1_ref[...]
    gl_ref[...] = l0_ref[0] + l1_ref[...]


def whole(shape):
    return pl.BlockSpec(shape, lambda n: (0,) * len(shape))


def call(kernel, ins, outs, scratch, flops, nbytes, steps=4, limit=40):
    return pl.pallas_call(
        kernel,
        grid=(steps,),
        in_specs=ins,
        out_specs=[spec for _, _, spec in outs],
        out_shape=[pltpu.HBM(s, d) if d == BF16 else jax.ShapeDtypeStruct(s, d) for s, d, _ in outs],
        scratch_shapes=[pltpu.VMEM(s, d) for s, d in scratch],
        cost_estimate=pl.CostEstimate(flops=flops, bytes_accessed=nbytes, transcendentals=0),
        compiler_params=pltpu.CompilerParams(vmem_limit_bytes=limit << 20),
    )


RIGHT = whole((16, 4, JE))
WEIGHT = whole((CE, Z))
ANY = pl.BlockSpec(memory_space=pl.ANY)
VM = pl.BlockSpec(memory_space=pltpu.VMEM)
DMA = pltpu.SemaphoreType.DMA


def flat_call(kernel, ins, outs, scratch, sems, flops, nbytes):
    return pl.pallas_call(
        kernel,
        in_specs=ins,
        out_specs=[spec for _, spec in outs],
        out_shape=[shape for shape, _ in outs],
        scratch_shapes=[pltpu.VMEM(s, d) for s, d in scratch] + [DMA(s) for s in sems],
        cost_estimate=pl.CostEstimate(flops=flops, bytes_accessed=nbytes, transcendentals=0),
        compiler_params=pltpu.CompilerParams(vmem_limit_bytes=40 << 20),
    )


GR_PART = (jax.ShapeDtypeStruct((4, 4, 4, JE), F32), VM)
grads_call = flat_call(
    grads_kernel,
    [VM] * 4 + [ANY] * 2,
    [(pltpu.HBM((IC, JE), BF16), ANY)] * 2 + [GR_PART] * 2
    + [(jax.ShapeDtypeStruct((IC, 3 * S), BF16), VM), (jax.ShapeDtypeStruct((IJ, 2 * Z), BF16), VM), (jax.ShapeDtypeStruct((8, Z), F32), VM)],
    [((S, IC), F32), ((2 * S, IC), BF16), ((IJ, Z), F32), ((CE, Z), F32), ((CE, Z), F32), ((CE, 3 * Z), BF16),
     ((CE, 256), F32), ((IC, JE), BF16), ((IC, JE), BF16), ((JE, S), F32)],
    [(2,), (2, 4)],
    2 * 10**9, 6 << 20)
GW_PART = (jax.ShapeDtypeStruct((16, 40, Z), F32), VM)
outer_call = flat_call(
    outer_kernel,
    [VM] * 5,
    [(pltpu.HBM((4, CE, 256), BF16), ANY)] * 2 + [(pltpu.HBM((JE, 2 * S), BF16), ANY)] + [GW_PART] * 2,
    [((S, JE), F32), ((JE, S), F32), ((JE, 3 * S), BF16), ((IC, 256), F32), ((IC, 256), F32), ((4, CE, 256), BF16), ((4, CE, 256), BF16), ((CE, Z), F32)],
    [(1,), (2, 4)],
    2 * 10**9, 7 << 20)
pair_call = flat_call(
    pair_kernel,
    [ANY] * 3 + [VM],
    [(pltpu.HBM((IJ, Z), F32), ANY)],
    [((4, CE, 256), BF16), ((4, CE, 256), BF16), ((CE, Z), F32), ((CE, Z), F32), ((2 * Z, CE), BF16), ((IJ, Z), F32)],
    [(1,), (2, 4), (4,)],
    10**9, 5 << 20)
grad_left_call = flat_call(
    grad_left_kernel,
    [ANY] * 3,
    [(jax.ShapeDtypeStruct((4, 2, 16, IC), F32), VM)],
    [((IC, JE), BF16), ((IC, JE), BF16), ((JE, 2 * S), BF16), ((S, IC), F32)],
    [(1,), (2, 4)],
    10**9, 6 << 20)
join_call = call(
    join_kernel,
    [whole((16, C, Z))] * 2 + [whole((2, 4, JE)), whole((4, JE)), whole((2, 16, IC)), whole((16, IC))],
    [((CE, Z), F32, WEIGHT), ((4, JE), F32, whole((4, JE))), ((16, IC), F32, whole((16, IC)))],
    [], 10**5, 1 << 20, 1, 8)
copies_call = call(copies_kernel, [whole((4, JE))], [((16, 4, JE), F32, RIGHT)], [], 10**5, 1 << 19, 1, 8)
spread_call = call(sum_spread_kernel, [whole((16, 40, Z))], [((8, 40, Z), F32, whole((8, 40, Z)))], [], 10**5, 1 << 19, 1, 8)
final_call = call(
    sum_final_kernel,
    [whole((8, 40, Z))],
    [((16, C, Z), F32, whole((16, C, Z))), ((1, Z), F32, whole((1, Z)))],
    [], 10**5, 1 << 19, 1, 8)


def rid(z, y, c):
    return (z * 4 + y) * 2 + c


CORE = [(r, r ^ 1) for r in range(32)]
YZ = [[rid(z, y, c) for z in range(4) for y in range(4)] for c in range(2)]
XY = [[rid(z, y, c) * 8 + h * 4 + x for y in range(4) for x in range(4)] for z in range(4) for h in range(2) for c in range(2)]
Z8 = [[rid(z, y, c) * 8 + h * 4 + x for z in range(4) for h in range(2)] for y in range(4) for x in range(4) for c in range(2)]
BOTH = ("row", "col")
R4 = range(4)
Y_FLIP = {k: [(rid(z, y, c), rid(z, y ^ k, c)) for z in R4 for y in R4 for c in range(2)] for k in (1, 3)}
Z_FLIP = {k: [(rid(z, y, c), rid(z ^ k, y, c)) for z in R4 for y in R4 for c in range(2)] for k in (1, 3)}
X_FLIP = {k: [(q, q ^ k) for q in range(8)] for k in (1, 3)}
X_PERMS = [[(h * 4 + x, h * 4 + (x + k) % 4) for h in range(2) for x in R4] for k in (1, 2, 3)]
H_PERM = [(q, q ^ 4) for q in range(8)]


def in_hbm(*xs):
    return [pltpu.with_memory_space_constraint(x, pltpu.HBM) for x in xs]


def body(left, right, w_out, b_out, pair_grad):
    tie = lax.optimization_barrier
    g = pair_grad.reshape(IJ, Z)
    left_far = lax.ppermute(left, "col", H_PERM)
    (copies,) = copies_call(*in_hbm(right))
    right_own = lax.all_to_all(copies, "row", 0, 0, axis_index_groups=YZ)
    left_pair = jnp.stack([left, left_far])
    pieces = [left_pair] + [lax.ppermute(left_pair, "col", p) for p in X_PERMS]
    goh, gol, gr_own, gr_other, left_parts, g_parts, bias = grads_call(*pieces, *in_hbm(g, w_out))
    right_other = lax.ppermute(right_own, "row", CORE)
    oh, ol, bc, gw_own, gw_other = outer_call(left_parts, g_parts, bias, right_own, right_other)
    gw = gw_own + lax.ppermute(gw_other, "row", CORE)
    gw, goh, gol, bc = tie((gw, goh, gol, bc))
    gw = lax.all_to_all(gw, BOTH, 0, 0, axis_index_groups=XY)
    gr = gr_own + lax.ppermute(gr_other, "row", CORE)
    (gl,) = grad_left_call(*in_hbm(goh, gol, bc))
    (gw,) = spread_call(gw)
    gw, oh, ol = tie((gw, oh, ol))
    gr = gr[:2] + lax.ppermute(gr[2:], "row", Y_FLIP[1])
    gr = gr[0] + lax.ppermute(gr[1], "row", Y_FLIP[3])
    gl = gl[:2] + lax.ppermute(gl[2:], "col", X_FLIP[1])
    gl = gl[0] + lax.ppermute(gl[1], "col", X_FLIP[3])
    gw = lax.all_to_all(gw, BOTH, 0, 0, axis_index_groups=Z8)
    (pair_out,) = pair_call(*in_hbm(oh, ol, w_out), b_out.reshape(1, Z))
    gw, grad_bias = final_call(gw)
    gr = gr[:2] + lax.ppermute(gr[2:], "row", Z_FLIP[1])
    gr_part = lax.ppermute(gr[1], "row", Z_FLIP[3])
    gl_part = lax.ppermute(gl[1], "col", H_PERM)
    gw_own = lax.all_to_all(gw, BOTH, 0, 0, axis_index_groups=XY)
    gw_other = lax.ppermute(gw_own, "row", CORE)
    grad_weight, grad_right, grad_left = join_call(gw_own, gw_other, gr, gr_part, gl, gl_part)
    return (pair_out.reshape(TI, TJ, Z), grad_left, grad_right, grad_weight, grad_bias.reshape(Z))


def solution(mesh):
    placed = (P("col", "row"), P("row", "col"), P(), P(), P("row", "col", None))
    return jax.shard_map(
        body,
        mesh=mesh,
        in_specs=placed,
        out_specs=(P("row", "col", None), P("col", "row"), P("row", "col"), P(), P()),
        check_vma=False,
    )
```

```python
import functools

import jax
import jax.numpy as jnp
from jax import lax
from jax.experimental import pallas as pl
from jax.experimental.pallas import tpu as pltpu
from jax.sharding import PartitionSpec as P


C = 32
Z = 128
S = 128
TI = 16
TJ = 64
IC = TI * C
JE = TJ * C
IJ = TI * TJ
CE = C * C
F32 = jnp.float32
BF16 = jnp.bfloat16
NT = (((1,), (1,)), ((), ()))
NN = (((1,), (0,)), ((), ()))


def split(x):
    hi = x.astype(BF16)
    return hi, (x - hi.astype(F32)).astype(BF16)


def dot(x, y, dims=NN):
    return lax.dot_general(x, y, dims, preferred_element_type=F32)


def half_swap(x0, x1):
    lane = lax.broadcasted_iota(jnp.int32, x0.shape, 1)
    low = lane < 64
    r0 = pltpu.roll(x0, 64, 1)
    r1 = pltpu.roll(x1, 64, 1)
    return jnp.where(low, x0, r1), jnp.where(low, r0, x1)


def core_index():
    return lax.rem(lax.axis_index("row"), 2)


def load_left(piece_refs, a_scr):
    core = core_index()
    col = lax.axis_index("col")
    for p, ref in enumerate(piece_refs):
        for h, half in ((0, col // 4), (1, 1 - col // 4)):
            q = half * 4 + lax.rem(col + 4 - p, 4)
            x = ref[h]
            lo = jnp.concatenate([x[0:4], x[8:12]], axis=0)
            hi = jnp.concatenate([x[4:8], x[12:16]], axis=0)
            a_scr[pl.ds(pl.multiple_of(q * 8, 8), 8), :] = jnp.where(core == 0, lo, hi)
            a_scr[pl.ds(pl.multiple_of(64 + q * 8, 8), 8), :] = jnp.where(core == 0, hi, lo)


def load_weight(w_ref, wp_scr):
    for e in range(C):
        wp_scr[C * e : C * e + C, :] = w_ref[pl.ds(e, C, stride=C), :]


def slot_of(k):
    return jnp.where(k == 0, 0, jnp.where(k == 3, 1, k + 1))


def grads_kernel(l0_ref, l1_ref, l2_ref, l3_ref, g_hbm, w_hbm, goh_hbm, gol_hbm, own_ref, other_ref,
                 at_ref, gc_ref, bias_ref, a_scr, ac_scr, g_scr, w_scr, wp_scr, wc_scr, r_scr, goh_scr, gol_scr, t_scr, in_sem, out_sem):
    get_w = pltpu.make_async_copy(w_hbm, w_scr, in_sem.at[0])
    get_g = pltpu.make_async_copy(g_hbm, g_scr, in_sem.at[1])
    get_w.start()
    get_g.start()
    load_left((l0_ref, l1_ref, l2_ref, l3_ref), a_scr)
    ah, al = split(a_scr[...])
    ac_scr[0:S, :] = ah
    ac_scr[S : 2 * S, :] = al
    ath, atl = split(a_scr[...].T)
    at_ref[:, 0:S] = ath
    at_ref[:, S : 2 * S] = atl
    at_ref[:, 2 * S : 3 * S] = ath
    get_w.wait()
    load_weight(w_scr, wp_scr)
    wh, wl = split(wp_scr[...])
    wc_scr[:, 0:Z] = wh
    wc_scr[:, Z : 2 * Z] = wl
    wc_scr[:, 2 * Z : 3 * Z] = wh
    get_g.wait()
    bias_ref[...] = jnp.broadcast_to(jnp.sum(g_scr[...], axis=0, keepdims=True), (8, Z))

    def puts(n):
        rows = pl.ds(pl.multiple_of(n * 128, 128), 128)
        return (
            pltpu.make_async_copy(goh_scr.at[rows, :], goh_hbm.at[rows, :], out_sem.at[0, n]),
            pltpu.make_async_copy(gol_scr.at[rows, :], gol_hbm.at[rows, :], out_sem.at[1, n]),
        )

    @pl.loop(0, 4)
    def _(n):
        part = pl.ds(pl.multiple_of(n * 256, 256), 256)
        gh, gl = split(g_scr[part, :])
        gc_ref[part, 0:Z] = gh
        gc_ref[part, Z : 2 * Z] = gl
        r_scr[...] = dot(wc_scr[...], jnp.concatenate([gh, gh, gl], axis=1), NT)
        for ip in range(2):
            for ep in range(16):
                x0 = r_scr[64 * ep : 64 * ep + 32, 128 * ip : 128 * ip + 128]
                x1 = r_scr[64 * ep + 32 : 64 * ep + 64, 128 * ip : 128 * ip + 128]
                for k, y in enumerate(half_swap(x0, x1)):
                    hi, lo = split(y)
                    rows = pl.ds(pl.multiple_of((4 * n + 2 * ip + k) * C, C), C)
                    goh_scr[rows, 128 * ep : 128 * ep + 128] = hi
                    gol_scr[rows, 128 * ep : 128 * ep + 128] = lo
        for put in puts(n):
            put.start()

    @pl.loop(0, 8)
    def _(n):
        cols = pl.ds(pl.multiple_of(n * 256, 256), 256)
        r = dot(ac_scr[...], goh_scr[:, cols])
        r = r[:S] + r[S:] + dot(ac_scr[0:S, :], gol_scr[:, cols])
        t_scr[cols, :] = (r * (1.0 / S)).T

    row = lax.axis_index("row") // 2
    y = lax.rem(row, 4)
    z = row // 4
    for m in range(16):
        block = jnp.concatenate([t_scr[pl.ds(4 * m + q, C, stride=TJ), :] for q in range(4)], axis=0)
        block = block.T
        for k in range(16):
            yy = slot_of((k % 4) ^ y)
            zz = slot_of((k // 4) ^ z)
            own_ref[zz, yy, :, 128 * m : 128 * m + 128] = block[4 * k : 4 * k + 4]
            other_ref[zz, yy, :, 128 * m : 128 * m + 128] = block[64 + 4 * k : 68 + 4 * k]
    for n in range(4):
        for put in puts(n):
            put.wait()


def outer_kernel(at_ref, gc_ref, bias_ref, own_ref, other_ref, oh_hbm, ol_hbm, bc_hbm, gwo_ref, gwx_ref,
                 b_scr, t_scr, bc_scr, r0_scr, r1_scr, oh_scr, ol_scr, w_scr, b_sem, o_sem):
    for k in range(16):
        b_scr[4 * k : 4 * k + 4, :] = own_ref[k]
        b_scr[64 + 4 * k : 68 + 4 * k, :] = other_ref[k]
    for m in range(16):
        t_scr[128 * m : 128 * m + 128, :] = b_scr[:, 128 * m : 128 * m + 128].T
    for e in range(C):
        hi, lo = split(t_scr[pl.ds(e, TJ, stride=C), :])
        rows = slice(TJ * e, TJ * e + TJ)
        bc_scr[rows, 0:S] = hi
        bc_scr[rows, S : 2 * S] = hi
        bc_scr[rows, 2 * S : 3 * S] = lo
    puts = [pltpu.make_async_copy(bc_scr.at[:, S : 3 * S], bc_hbm, b_sem.at[0])]
    puts[0].start()
    r_scr = (r0_scr, r1_scr)

    def multiply(n):
        r_scr[n % 2][...] = dot(at_ref[...], bc_scr[256 * n : 256 * n + 256, :], NT)

    def weigh(m):
        rows = slice(512 * m, 512 * m + 512)
        hi = jnp.concatenate([oh_scr[q, rows, :] for q in range(4)], axis=1)
        lo = jnp.concatenate([ol_scr[q, rows, :] for q in range(4)], axis=1)
        r = dot(hi, gc_ref[...])
        w_scr[rows, :] = (r[:, :Z] + r[:, Z:] + dot(lo, gc_ref[:, 0:Z])) * (1.0 / S)

    multiply(0)
    for n in range(8):
        if n < 7:
            multiply(n + 1)
        if n == 4:
            weigh(0)
        for ep in range(2):
            for ip in range(8):
                x0 = r_scr[n % 2][64 * ip : 64 * ip + 32, 128 * ep : 128 * ep + 128]
                x1 = r_scr[n % 2][64 * ip + 32 : 64 * ip + 64, 128 * ep : 128 * ep + 128]
                for k, y in enumerate(half_swap(x0, x1)):
                    hi, lo = split(y)
                    row = (4 * n + 2 * ep + k) * C
                    cols = slice(128 * (ip % 2), 128 * (ip % 2) + 128)
                    oh_scr[ip // 2, row : row + C, cols] = hi
                    ol_scr[ip // 2, row : row + C, cols] = lo
        if n % 2 == 1:
            rows = slice(128 * (n - 1), 128 * (n + 1))
            for i, (src, dst) in enumerate(((oh_scr, oh_hbm), (ol_scr, ol_hbm))):
                put = pltpu.make_async_copy(src.at[:, rows, :], dst.at[:, rows, :], o_sem.at[i, n // 2])
                put.start()
                puts.append(put)
    weigh(1)
    core = core_index()
    for k in range(16):
        lo = w_scr[pl.ds(k, C, stride=C), :]
        hi = w_scr[pl.ds(16 + k, C, stride=C), :]
        gwo_ref[k, 0:C, :] = jnp.where(core == 0, lo, hi)
        gwx_ref[k, 0:C, :] = jnp.where(core == 0, hi, lo)
        gwo_ref[k, C : C + 8, :] = bias_ref[...]
        gwx_ref[k, C : C + 8, :] = bias_ref[...]
    for put in puts:
        put.wait()


def pair_kernel(first, oh_hbm, ol_hbm, w_hbm, b_ref, *refs):
    p_hbm, oh_scr, ol_scr, w_scr, wp_scr, wc_scr, p_scr, w_sem, in_sem, out_sem = refs[-10:]
    get_w = pltpu.make_async_copy(w_hbm, w_scr, w_sem.at[0])
    get_w.start()
    gets = []
    for n in range(2):
        for i, (src, dst) in enumerate(((oh_hbm, oh_scr), (ol_hbm, ol_scr))):
            get = pltpu.make_async_copy(src.at[first + n], dst.at[n], in_sem.at[i, n])
            get.start()
            gets.append(get)
    get_w.wait()
    load_weight(w_scr, wp_scr)
    wth, wtl = split(wp_scr[...].T)
    wc_scr[0:Z, :] = wth
    wc_scr[Z : 2 * Z, :] = wtl
    puts = []
    for n in range(2):
        for get in gets[2 * n : 2 * n + 2]:
            get.wait()
        r = dot(wc_scr[...], oh_scr[n])
        r = r[:Z] + r[Z:] + dot(wc_scr[0:Z, :], ol_scr[n])
        p_scr[256 * n : 256 * n + 256, :] = (r * (1.0 / S)).T + b_ref[...]
        put = pltpu.make_async_copy(
            p_scr.at[256 * n : 256 * n + 256, :],
            p_hbm.at[256 * (first + n) : 256 * (first + n) + 256, :], out_sem.at[n])
        put.start()
        puts.append(put)
    for put in puts:
        put.wait()


def grad_left_kernel(goh_hbm, gol_hbm, bc_hbm, gl_ref, goh_scr, gol_scr, bc_scr, s_scr, b_sem, in_sem):
    get_b = pltpu.make_async_copy(bc_hbm, bc_scr, b_sem.at[0])
    get_b.start()
    gets = []
    for n in range(4):
        rows = slice(128 * n, 128 * n + 128)
        for i, (src, dst) in enumerate(((goh_hbm, goh_scr), (gol_hbm, gol_scr))):
            get = pltpu.make_async_copy(src.at[rows, :], dst.at[rows, :], in_sem.at[i, n])
            get.start()
            gets.append(get)
    get_b.wait()
    for get in gets:
        get.wait()
    r = dot(goh_scr[...], bc_scr[...])
    s_scr[...] = ((r[:, :S] + r[:, S:] + dot(gol_scr[...], bc_scr[:, 0:S])) * (1.0 / S)).T
    core = core_index()
    col = lax.axis_index("col")
    for q in range(8):
        own = s_scr[8 * q : 8 * q + 8, :]
        other = s_scr[64 + 8 * q : 72 + 8 * q, :]
        lo = jnp.where(core == 0, own, other)
        hi = jnp.where(core == 0, other, own)
        xx = slot_of((q % 4) ^ lax.rem(col, 4))
        zz = lax.rem(q // 4 + 2 - col // 4, 2)
        gl_ref[xx, zz, 0:8, :] = jnp.concatenate([lo[0:4], hi[0:4]], axis=0)
        gl_ref[xx, zz, 8:16, :] = jnp.concatenate([lo[4:8], hi[4:8]], axis=0)


def copies_kernel(x_ref, out_ref):
    for k in range(out_ref.shape[0]):
        out_ref[k] = x_ref[...]


def sum_spread_kernel(x_ref, out_ref):
    total = x_ref[0]
    for k in range(1, x_ref.shape[0]):
        total = total + x_ref[k]
    for k in range(out_ref.shape[0]):
        out_ref[k] = total


def sum_final_kernel(x_ref, out_ref, bias_ref):
    total = x_ref[0]
    for k in range(1, x_ref.shape[0]):
        total = total + x_ref[k]
    total = total * (1.0 / 512)
    for k in range(out_ref.shape[0]):
        out_ref[k] = total[:C]
    bias_ref[...] = total[C : C + 1]


def join_kernel(own_ref, other_ref, r0_ref, r1_ref, l0_ref, l1_ref, w_ref, gr_ref, gl_ref):
    core = core_index()
    for k in range(16):
        own = own_ref[k]
        other = other_ref[k]
        w_ref[C * k : C * k + C, :] = jnp.where(core == 0, own, other)
        w_ref[512 + C * k : 512 + C * k + C, :] = jnp.where(core == 0, other, own)
    gr_ref[...] = r0_ref[0] + r1_ref[...]
    gl_ref[...] = l0_ref[0] + l1_ref[...]


def whole(shape):
    return pl.BlockSpec(shape, lambda n: (0,) * len(shape))


def call(kernel, ins, outs, scratch, flops, nbytes, steps=4, limit=40):
    return pl.pallas_call(
        kernel,
        grid=(steps,),
        in_specs=ins,
        out_specs=[spec for _, _, spec in outs],
        out_shape=[pltpu.HBM(s, d) if d == BF16 else jax.ShapeDtypeStruct(s, d) for s, d, _ in outs],
        scratch_shapes=[pltpu.VMEM(s, d) for s, d in scratch],
        cost_estimate=pl.CostEstimate(flops=flops, bytes_accessed=nbytes, transcendentals=0),
        compiler_params=pltpu.CompilerParams(vmem_limit_bytes=limit << 20),
    )


RIGHT = whole((16, 4, JE))
WEIGHT = whole((CE, Z))
ANY = pl.BlockSpec(memory_space=pl.ANY)
VM = pl.BlockSpec(memory_space=pltpu.VMEM)
DMA = pltpu.SemaphoreType.DMA


def flat_call(kernel, ins, outs, scratch, sems, flops, nbytes, alias=None):
    return pl.pallas_call(
        kernel,
        in_specs=ins,
        out_specs=[spec for _, spec in outs],
        out_shape=[shape for shape, _ in outs],
        scratch_shapes=[pltpu.VMEM(s, d) for s, d in scratch] + [DMA(s) for s in sems],
        input_output_aliases=alias or {},
        cost_estimate=pl.CostEstimate(flops=flops, bytes_accessed=nbytes, transcendentals=0),
        compiler_params=pltpu.CompilerParams(vmem_limit_bytes=40 << 20),
    )


GR_PART = (jax.ShapeDtypeStruct((4, 4, 4, JE), F32), VM)
grads_call = flat_call(
    grads_kernel,
    [VM] * 4 + [ANY] * 2,
    [(pltpu.HBM((IC, JE), BF16), ANY)] * 2 + [GR_PART] * 2
    + [(jax.ShapeDtypeStruct((IC, 3 * S), BF16), VM), (jax.ShapeDtypeStruct((IJ, 2 * Z), BF16), VM), (jax.ShapeDtypeStruct((8, Z), F32), VM)],
    [((S, IC), F32), ((2 * S, IC), BF16), ((IJ, Z), F32), ((CE, Z), F32), ((CE, Z), F32), ((CE, 3 * Z), BF16),
     ((CE, 256), F32), ((IC, JE), BF16), ((IC, JE), BF16), ((JE, S), F32)],
    [(2,), (2, 4)],
    2 * 10**9, 6 << 20)
GW_PART = (jax.ShapeDtypeStruct((16, 40, Z), F32), VM)
outer_call = flat_call(
    outer_kernel,
    [VM] * 5,
    [(pltpu.HBM((4, CE, 256), BF16), ANY)] * 2 + [(pltpu.HBM((JE, 2 * S), BF16), ANY)] + [GW_PART] * 2,
    [((S, JE), F32), ((JE, S), F32), ((JE, 3 * S), BF16), ((IC, 256), F32), ((IC, 256), F32), ((4, CE, 256), BF16), ((4, CE, 256), BF16), ((CE, Z), F32)],
    [(1,), (2, 4)],
    2 * 10**9, 7 << 20)
pair_calls = [
    flat_call(
        functools.partial(pair_kernel, first),
        [ANY] * 3 + [VM] + [ANY] * (first // 2),
        [(pltpu.HBM((IJ, Z), F32), ANY)],
        [((2, CE, 256), BF16), ((2, CE, 256), BF16), ((CE, Z), F32), ((CE, Z), F32), ((2 * Z, CE), BF16), ((512, Z), F32)],
        [(1,), (2, 2), (2,)],
        5 * 10**8, 3 << 20, {4: 0} if first else None)
    for first in (0, 2)
]
grad_left_call = flat_call(
    grad_left_kernel,
    [ANY] * 3,
    [(jax.ShapeDtypeStruct((4, 2, 16, IC), F32), VM)],
    [((IC, JE), BF16), ((IC, JE), BF16), ((JE, 2 * S), BF16), ((S, IC), F32)],
    [(1,), (2, 4)],
    10**9, 6 << 20)
join_call = call(
    join_kernel,
    [whole((16, C, Z))] * 2 + [whole((2, 4, JE)), whole((4, JE)), whole((2, 16, IC)), whole((16, IC))],
    [((CE, Z), F32, WEIGHT), ((4, JE), F32, whole((4, JE))), ((16, IC), F32, whole((16, IC)))],
    [], 10**5, 1 << 20, 1, 8)
copies_call = call(copies_kernel, [whole((4, JE))], [((16, 4, JE), F32, RIGHT)], [], 10**5, 1 << 19, 1, 8)
spread_call = call(sum_spread_kernel, [whole((16, 40, Z))], [((8, 40, Z), F32, whole((8, 40, Z)))], [], 10**5, 1 << 19, 1, 8)
final_call = call(
    sum_final_kernel,
    [whole((8, 40, Z))],
    [((16, C, Z), F32, whole((16, C, Z))), ((1, Z), F32, whole((1, Z)))],
    [], 10**5, 1 << 19, 1, 8)


def rid(z, y, c):
    return (z * 4 + y) * 2 + c


CORE = [(r, r ^ 1) for r in range(32)]
YZ = [[rid(z, y, c) for z in range(4) for y in range(4)] for c in range(2)]
XY = [[rid(z, y, c) * 8 + h * 4 + x for y in range(4) for x in range(4)] for z in range(4) for h in range(2) for c in range(2)]
Z8 = [[rid(z, y, c) * 8 + h * 4 + x for z in range(4) for h in range(2)] for y in range(4) for x in range(4) for c in range(2)]
BOTH = ("row", "col")
R4 = range(4)
Y_FLIP = {k: [(rid(z, y, c), rid(z, y ^ k, c)) for z in R4 for y in R4 for c in range(2)] for k in (1, 3)}
Z_FLIP = {k: [(rid(z, y, c), rid(z ^ k, y, c)) for z in R4 for y in R4 for c in range(2)] for k in (1, 3)}
X_FLIP = {k: [(q, q ^ k) for q in range(8)] for k in (1, 3)}
X_PERMS = [[(h * 4 + x, h * 4 + (x + k) % 4) for h in range(2) for x in R4] for k in (1, 2, 3)]
H_PERM = [(q, q ^ 4) for q in range(8)]


def in_hbm(*xs):
    return [pltpu.with_memory_space_constraint(x, pltpu.HBM) for x in xs]


def body(left, right, w_out, b_out, pair_grad):
    tie = lax.optimization_barrier
    g = pair_grad.reshape(IJ, Z)
    left_far = lax.ppermute(left, "col", H_PERM)
    (copies,) = copies_call(*in_hbm(right))
    right_own = lax.all_to_all(copies, "row", 0, 0, axis_index_groups=YZ)
    left_pair = jnp.stack([left, left_far])
    pieces = [left_pair] + [lax.ppermute(left_pair, "col", p) for p in X_PERMS]
    goh, gol, gr_own, gr_other, left_parts, g_parts, bias = grads_call(*pieces, *in_hbm(g, w_out))
    right_other = lax.ppermute(right_own, "row", CORE)
    oh, ol, bc, gw_own, gw_other = outer_call(left_parts, g_parts, bias, right_own, right_other)
    gw = gw_own + lax.ppermute(gw_other, "row", CORE)
    gw, goh, gol, bc = tie((gw, goh, gol, bc))
    gw = lax.all_to_all(gw, BOTH, 0, 0, axis_index_groups=XY)
    gr = gr_own + lax.ppermute(gr_other, "row", CORE)
    (gl,) = grad_left_call(*in_hbm(goh, gol, bc))
    (gw,) = spread_call(gw)
    gw, oh, ol = tie((gw, oh, ol))
    gr = gr[:2] + lax.ppermute(gr[2:], "row", Z_FLIP[1])
    gr = gr[0] + lax.ppermute(gr[1], "row", Z_FLIP[3])
    gl = gl[:2] + lax.ppermute(gl[2:], "col", X_FLIP[1])
    gl = gl[0] + lax.ppermute(gl[1], "col", X_FLIP[3])
    gw = lax.all_to_all(gw, BOTH, 0, 0, axis_index_groups=Z8)
    (pair_half,) = pair_calls[0](*in_hbm(oh, ol, w_out), b_out.reshape(1, Z))
    (pair_out,) = pair_calls[1](*in_hbm(oh, ol, w_out), b_out.reshape(1, Z), pair_half)
    gw, grad_bias = final_call(gw)
    gr = gr[:2] + lax.ppermute(gr[2:], "row", Y_FLIP[1])
    gr_part = lax.ppermute(gr[1], "row", Y_FLIP[3])
    gl_part = lax.ppermute(gl[1], "col", H_PERM)
    gw_own = lax.all_to_all(gw, BOTH, 0, 0, axis_index_groups=XY)
    gw_other = lax.ppermute(gw_own, "row", CORE)
    grad_weight, grad_right, grad_left = join_call(gw_own, gw_other, gr, gr_part, gl, gl_part)
    return (pair_out.reshape(TI, TJ, Z), grad_left, grad_right, grad_weight, grad_bias.reshape(Z))


def solution(mesh):
    placed = (P("col", "row"), P("row", "col"), P(), P(), P("row", "col", None))
    return jax.shard_map(
        body,
        mesh=mesh,
        in_specs=placed,
        out_specs=(P("row", "col", None), P("col", "row"), P("row", "col"), P(), P()),
        check_vma=False,
    )
```

```python
import functools

import jax
import jax.numpy as jnp
from jax import lax
from jax.experimental import pallas as pl
from jax.experimental.pallas import tpu as pltpu
from jax.sharding import PartitionSpec as P


C = 32
Z = 128
S = 128
TI = 16
TJ = 64
IC = TI * C
JE = TJ * C
IJ = TI * TJ
CE = C * C
F32 = jnp.float32
BF16 = jnp.bfloat16
NT = (((1,), (1,)), ((), ()))
NN = (((1,), (0,)), ((), ()))


def split(x):
    hi = x.astype(BF16)
    return hi, (x - hi.astype(F32)).astype(BF16)


def dot(x, y, dims=NN):
    return lax.dot_general(x, y, dims, preferred_element_type=F32)


def half_swap(x0, x1):
    lane = lax.broadcasted_iota(jnp.int32, x0.shape, 1)
    low = lane < 64
    r0 = pltpu.roll(x0, 64, 1)
    r1 = pltpu.roll(x1, 64, 1)
    return jnp.where(low, x0, r1), jnp.where(low, r0, x1)


def core_index():
    return lax.rem(lax.axis_index("row"), 2)


def load_left(piece_refs, a_scr):
    core = core_index()
    col = lax.axis_index("col")
    for p, ref in enumerate(piece_refs):
        for h, half in ((0, col // 4), (1, 1 - col // 4)):
            q = half * 4 + lax.rem(col + 4 - p, 4)
            x = ref[h]
            lo = jnp.concatenate([x[0:4], x[8:12]], axis=0)
            hi = jnp.concatenate([x[4:8], x[12:16]], axis=0)
            a_scr[pl.ds(pl.multiple_of(q * 8, 8), 8), :] = jnp.where(core == 0, lo, hi)
            a_scr[pl.ds(pl.multiple_of(64 + q * 8, 8), 8), :] = jnp.where(core == 0, hi, lo)


def load_weight(w_ref, wp_scr):
    for e in range(C):
        wp_scr[C * e : C * e + C, :] = w_ref[pl.ds(e, C, stride=C), :]


def slot_of(k):
    return jnp.where(k == 0, 0, jnp.where(k == 3, 1, k + 1))


def grads_kernel(l0_ref, l1_ref, l2_ref, l3_ref, g_hbm, w_hbm, goh_hbm, gol_hbm, own_ref, other_ref,
                 at_ref, gc_ref, bias_ref, a_scr, ac_scr, g_scr, w_scr, wp_scr, wc_scr, r_scr, goh_scr, gol_scr, t_scr, in_sem, out_sem):
    get_w = pltpu.make_async_copy(w_hbm, w_scr, in_sem.at[0])
    get_g = pltpu.make_async_copy(g_hbm, g_scr, in_sem.at[1])
    get_w.start()
    get_g.start()
    load_left((l0_ref, l1_ref, l2_ref, l3_ref), a_scr)
    ah, al = split(a_scr[...])
    ac_scr[0:S, :] = ah
    ac_scr[S : 2 * S, :] = al
    ath, atl = split(a_scr[...].T)
    at_ref[:, 0:S] = ath
    at_ref[:, S : 2 * S] = atl
    at_ref[:, 2 * S : 3 * S] = ath
    get_w.wait()
    load_weight(w_scr, wp_scr)
    wh, wl = split(wp_scr[...])
    wc_scr[:, 0:Z] = wh
    wc_scr[:, Z : 2 * Z] = wl
    wc_scr[:, 2 * Z : 3 * Z] = wh
    get_g.wait()
    bias_ref[...] = jnp.broadcast_to(jnp.sum(g_scr[...], axis=0, keepdims=True), (8, Z))

    def puts(n):
        rows = pl.ds(pl.multiple_of(n * 128, 128), 128)
        return (
            pltpu.make_async_copy(goh_scr.at[rows, :], goh_hbm.at[rows, :], out_sem.at[0, n]),
            pltpu.make_async_copy(gol_scr.at[rows, :], gol_hbm.at[rows, :], out_sem.at[1, n]),
        )

    @pl.loop(0, 4)
    def _(n):
        part = pl.ds(pl.multiple_of(n * 256, 256), 256)
        gh, gl = split(g_scr[part, :])
        gc_ref[part, 0:Z] = gh
        gc_ref[part, Z : 2 * Z] = gl
        r_scr[...] = dot(wc_scr[...], jnp.concatenate([gh, gh, gl], axis=1), NT)
        for ip in range(2):
            for ep in range(16):
                x0 = r_scr[64 * ep : 64 * ep + 32, 128 * ip : 128 * ip + 128]
                x1 = r_scr[64 * ep + 32 : 64 * ep + 64, 128 * ip : 128 * ip + 128]
                for k, y in enumerate(half_swap(x0, x1)):
                    hi, lo = split(y)
                    rows = pl.ds(pl.multiple_of((4 * n + 2 * ip + k) * C, C), C)
                    goh_scr[rows, 128 * ep : 128 * ep + 128] = hi
                    gol_scr[rows, 128 * ep : 128 * ep + 128] = lo
        for put in puts(n):
            put.start()

    @pl.loop(0, 8)
    def _(n):
        cols = pl.ds(pl.multiple_of(n * 256, 256), 256)
        r = dot(ac_scr[...], goh_scr[:, cols])
        r = r[:S] + r[S:] + dot(ac_scr[0:S, :], gol_scr[:, cols])
        t_scr[cols, :] = (r * (1.0 / S)).T

    row = lax.axis_index("row") // 2
    y = lax.rem(row, 4)
    z = row // 4
    for m in range(16):
        block = jnp.concatenate([t_scr[pl.ds(4 * m + q, C, stride=TJ), :] for q in range(4)], axis=0)
        block = block.T
        for k in range(16):
            yy = slot_of((k % 4) ^ y)
            zz = slot_of((k // 4) ^ z)
            own_ref[yy, zz, :, 128 * m : 128 * m + 128] = block[4 * k : 4 * k + 4]
            other_ref[yy, zz, :, 128 * m : 128 * m + 128] = block[64 + 4 * k : 68 + 4 * k]
    for n in range(4):
        for put in puts(n):
            put.wait()


def outer_kernel(at_ref, gc_ref, bias_ref, own_ref, other_ref, oh_hbm, ol_hbm, bc_hbm, gwo_ref, gwx_ref,
                 b_scr, t_scr, bc_scr, r0_scr, r1_scr, oh_scr, ol_scr, w_scr, b_sem, o_sem):
    for k in range(16):
        b_scr[4 * k : 4 * k + 4, :] = own_ref[k]
        b_scr[64 + 4 * k : 68 + 4 * k, :] = other_ref[k]
    for m in range(16):
        t_scr[128 * m : 128 * m + 128, :] = b_scr[:, 128 * m : 128 * m + 128].T
    for e in range(C):
        hi, lo = split(t_scr[pl.ds(e, TJ, stride=C), :])
        rows = slice(TJ * e, TJ * e + TJ)
        bc_scr[rows, 0:S] = hi
        bc_scr[rows, S : 2 * S] = hi
        bc_scr[rows, 2 * S : 3 * S] = lo
    puts = [pltpu.make_async_copy(bc_scr.at[:, S : 3 * S], bc_hbm, b_sem.at[0])]
    puts[0].start()
    r_scr = (r0_scr, r1_scr)

    def multiply(n):
        r_scr[n % 2][...] = dot(at_ref[...], bc_scr[256 * n : 256 * n + 256, :], NT)

    def weigh(m):
        rows = slice(512 * m, 512 * m + 512)
        hi = jnp.concatenate([oh_scr[q, rows, :] for q in range(4)], axis=1)
        lo = jnp.concatenate([ol_scr[q, rows, :] for q in range(4)], axis=1)
        r = dot(hi, gc_ref[...])
        w_scr[rows, :] = (r[:, :Z] + r[:, Z:] + dot(lo, gc_ref[:, 0:Z])) * (1.0 / S)

    multiply(0)
    for n in range(8):
        if n < 7:
            multiply(n + 1)
        if n == 4:
            weigh(0)
        for ep in range(2):
            for ip in range(8):
                x0 = r_scr[n % 2][64 * ip : 64 * ip + 32, 128 * ep : 128 * ep + 128]
                x1 = r_scr[n % 2][64 * ip + 32 : 64 * ip + 64, 128 * ep : 128 * ep + 128]
                for k, y in enumerate(half_swap(x0, x1)):
                    hi, lo = split(y)
                    row = (4 * n + 2 * ep + k) * C
                    cols = slice(128 * (ip % 2), 128 * (ip % 2) + 128)
                    oh_scr[ip // 2, row : row + C, cols] = hi
                    ol_scr[ip // 2, row : row + C, cols] = lo
        if n % 2 == 1:
            rows = slice(128 * (n - 1), 128 * (n + 1))
            for i, (src, dst) in enumerate(((oh_scr, oh_hbm), (ol_scr, ol_hbm))):
                put = pltpu.make_async_copy(src.at[:, rows, :], dst.at[:, rows, :], o_sem.at[i, n // 2])
                put.start()
                puts.append(put)
    weigh(1)
    core = core_index()
    for k in range(16):
        lo = w_scr[pl.ds(k, C, stride=C), :]
        hi = w_scr[pl.ds(16 + k, C, stride=C), :]
        gwo_ref[k, 0:C, :] = jnp.where(core == 0, lo, hi)
        gwx_ref[k, 0:C, :] = jnp.where(core == 0, hi, lo)
        gwo_ref[k, C : C + 8, :] = bias_ref[...]
        gwx_ref[k, C : C + 8, :] = bias_ref[...]
    for put in puts:
        put.wait()


def pair_kernel(first, oh_hbm, ol_hbm, w_hbm, b_ref, *refs):
    p_hbm, oh_scr, ol_scr, w_scr, wp_scr, wc_scr, p_scr, w_sem, in_sem, out_sem = refs[-10:]
    get_w = pltpu.make_async_copy(w_hbm, w_scr, w_sem.at[0])
    get_w.start()
    gets = []
    for n in range(2):
        for i, (src, dst) in enumerate(((oh_hbm, oh_scr), (ol_hbm, ol_scr))):
            get = pltpu.make_async_copy(src.at[first + n], dst.at[n], in_sem.at[i, n])
            get.start()
            gets.append(get)
    get_w.wait()
    load_weight(w_scr, wp_scr)
    wth, wtl = split(wp_scr[...].T)
    wc_scr[0:Z, :] = wth
    wc_scr[Z : 2 * Z, :] = wtl
    puts = []
    for n in range(2):
        for get in gets[2 * n : 2 * n + 2]:
            get.wait()
        r = dot(wc_scr[...], oh_scr[n])
        r = r[:Z] + r[Z:] + dot(wc_scr[0:Z, :], ol_scr[n])
        p_scr[256 * n : 256 * n + 256, :] = (r * (1.0 / S)).T + b_ref[...]
        put = pltpu.make_async_copy(
            p_scr.at[256 * n : 256 * n + 256, :],
            p_hbm.at[256 * (first + n) : 256 * (first + n) + 256, :], out_sem.at[n])
        put.start()
        puts.append(put)
    for put in puts:
        put.wait()


def grad_left_kernel(goh_hbm, gol_hbm, bc_hbm, gl_ref, goh_scr, gol_scr, bc_scr, s_scr, b_sem, in_sem):
    get_b = pltpu.make_async_copy(bc_hbm, bc_scr, b_sem.at[0])
    get_b.start()
    gets = []
    for n in range(4):
        rows = slice(128 * n, 128 * n + 128)
        for i, (src, dst) in enumerate(((goh_hbm, goh_scr), (gol_hbm, gol_scr))):
            get = pltpu.make_async_copy(src.at[rows, :], dst.at[rows, :], in_sem.at[i, n])
            get.start()
            gets.append(get)
    get_b.wait()
    for get in gets:
        get.wait()
    r = dot(goh_scr[...], bc_scr[...])
    s_scr[...] = ((r[:, :S] + r[:, S:] + dot(gol_scr[...], bc_scr[:, 0:S])) * (1.0 / S)).T
    core = core_index()
    col = lax.axis_index("col")
    for q in range(8):
        own = s_scr[8 * q : 8 * q + 8, :]
        other = s_scr[64 + 8 * q : 72 + 8 * q, :]
        lo = jnp.where(core == 0, own, other)
        hi = jnp.where(core == 0, other, own)
        xx = slot_of((q % 4) ^ lax.rem(col, 4))
        zz = lax.rem(q // 4 + 2 - col // 4, 2)
        gl_ref[xx, zz, 0:8, :] = jnp.concatenate([lo[0:4], hi[0:4]], axis=0)
        gl_ref[xx, zz, 8:16, :] = jnp.concatenate([lo[4:8], hi[4:8]], axis=0)


def copies_kernel(x_ref, out_ref):
    for k in range(out_ref.shape[0]):
        out_ref[k] = x_ref[...]


def sum_spread_kernel(x_ref, out_ref):
    total = x_ref[0]
    for k in range(1, x_ref.shape[0]):
        total = total + x_ref[k]
    for k in range(out_ref.shape[0]):
        out_ref[k] = total


def sum_final_kernel(x_ref, out_ref, bias_ref):
    total = x_ref[0]
    for k in range(1, x_ref.shape[0]):
        total = total + x_ref[k]
    total = total * (1.0 / 512)
    for k in range(out_ref.shape[0]):
        out_ref[k] = total[:C]
    bias_ref[...] = total[C : C + 1]


def join_kernel(own_ref, other_ref, r0_ref, r1_ref, l0_ref, l1_ref, w_ref, gr_ref, gl_ref):
    core = core_index()
    for k in range(16):
        own = own_ref[k]
        other = other_ref[k]
        w_ref[C * k : C * k + C, :] = jnp.where(core == 0, own, other)
        w_ref[512 + C * k : 512 + C * k + C, :] = jnp.where(core == 0, other, own)
    gr_ref[...] = r0_ref[0] + r1_ref[...]
    gl_ref[...] = l0_ref[0] + l1_ref[...]


def whole(shape):
    return pl.BlockSpec(shape, lambda n: (0,) * len(shape))


def call(kernel, ins, outs, scratch, flops, nbytes, steps=4, limit=40):
    return pl.pallas_call(
        kernel,
        grid=(steps,),
        in_specs=ins,
        out_specs=[spec for _, _, spec in outs],
        out_shape=[pltpu.HBM(s, d) if d == BF16 else jax.ShapeDtypeStruct(s, d) for s, d, _ in outs],
        scratch_shapes=[pltpu.VMEM(s, d) for s, d in scratch],
        cost_estimate=pl.CostEstimate(flops=flops, bytes_accessed=nbytes, transcendentals=0),
        compiler_params=pltpu.CompilerParams(vmem_limit_bytes=limit << 20),
    )


RIGHT = whole((16, 4, JE))
WEIGHT = whole((CE, Z))
ANY = pl.BlockSpec(memory_space=pl.ANY)
VM = pl.BlockSpec(memory_space=pltpu.VMEM)
DMA = pltpu.SemaphoreType.DMA


def flat_call(kernel, ins, outs, scratch, sems, flops, nbytes, alias=None):
    return pl.pallas_call(
        kernel,
        in_specs=ins,
        out_specs=[spec for _, spec in outs],
        out_shape=[shape for shape, _ in outs],
        scratch_shapes=[pltpu.VMEM(s, d) for s, d in scratch] + [DMA(s) for s in sems],
        input_output_aliases=alias or {},
        cost_estimate=pl.CostEstimate(flops=flops, bytes_accessed=nbytes, transcendentals=0),
        compiler_params=pltpu.CompilerParams(vmem_limit_bytes=40 << 20),
    )


GR_PART = (jax.ShapeDtypeStruct((4, 4, 4, JE), F32), VM)
grads_call = flat_call(
    grads_kernel,
    [VM] * 4 + [ANY] * 2,
    [(pltpu.HBM((IC, JE), BF16), ANY)] * 2 + [GR_PART] * 2
    + [(jax.ShapeDtypeStruct((IC, 3 * S), BF16), VM), (jax.ShapeDtypeStruct((IJ, 2 * Z), BF16), VM), (jax.ShapeDtypeStruct((8, Z), F32), VM)],
    [((S, IC), F32), ((2 * S, IC), BF16), ((IJ, Z), F32), ((CE, Z), F32), ((CE, Z), F32), ((CE, 3 * Z), BF16),
     ((CE, 256), F32), ((IC, JE), BF16), ((IC, JE), BF16), ((JE, S), F32)],
    [(2,), (2, 4)],
    2 * 10**9, 6 << 20)
GW_PART = (jax.ShapeDtypeStruct((16, 40, Z), F32), VM)
outer_call = flat_call(
    outer_kernel,
    [VM] * 5,
    [(pltpu.HBM((4, CE, 256), BF16), ANY)] * 2 + [(pltpu.HBM((JE, 2 * S), BF16), ANY)] + [GW_PART] * 2,
    [((S, JE), F32), ((JE, S), F32), ((JE, 3 * S), BF16), ((IC, 256), F32), ((IC, 256), F32), ((4, CE, 256), BF16), ((4, CE, 256), BF16), ((CE, Z), F32)],
    [(1,), (2, 4)],
    2 * 10**9, 7 << 20)
pair_calls = [
    flat_call(
        functools.partial(pair_kernel, first),
        [ANY] * 3 + [VM] + [ANY] * (first // 2),
        [(pltpu.HBM((IJ, Z), F32), ANY)],
        [((2, CE, 256), BF16), ((2, CE, 256), BF16), ((CE, Z), F32), ((CE, Z), F32), ((2 * Z, CE), BF16), ((512, Z), F32)],
        [(1,), (2, 2), (2,)],
        5 * 10**8, 3 << 20, {4: 0} if first else None)
    for first in (0, 2)
]
grad_left_call = flat_call(
    grad_left_kernel,
    [ANY] * 3,
    [(jax.ShapeDtypeStruct((4, 2, 16, IC), F32), VM)],
    [((IC, JE), BF16), ((IC, JE), BF16), ((JE, 2 * S), BF16), ((S, IC), F32)],
    [(1,), (2, 4)],
    10**9, 6 << 20)
join_call = call(
    join_kernel,
    [whole((16, C, Z))] * 2 + [whole((2, 4, JE)), whole((4, JE)), whole((2, 16, IC)), whole((16, IC))],
    [((CE, Z), F32, WEIGHT), ((4, JE), F32, whole((4, JE))), ((16, IC), F32, whole((16, IC)))],
    [], 10**5, 1 << 20, 1, 8)
copies_call = call(copies_kernel, [whole((4, JE))], [((16, 4, JE), F32, RIGHT)], [], 10**5, 1 << 19, 1, 8)
spread_call = call(sum_spread_kernel, [whole((16, 40, Z))], [((8, 40, Z), F32, whole((8, 40, Z)))], [], 10**5, 1 << 19, 1, 8)
final_call = call(
    sum_final_kernel,
    [whole((8, 40, Z))],
    [((16, C, Z), F32, whole((16, C, Z))), ((1, Z), F32, whole((1, Z)))],
    [], 10**5, 1 << 19, 1, 8)


def rid(z, y, c):
    return (z * 4 + y) * 2 + c


CORE = [(r, r ^ 1) for r in range(32)]
YZ = [[rid(z, y, c) for z in range(4) for y in range(4)] for c in range(2)]
XY = [[rid(z, y, c) * 8 + h * 4 + x for y in range(4) for x in range(4)] for z in range(4) for h in range(2) for c in range(2)]
Z8 = [[rid(z, y, c) * 8 + h * 4 + x for z in range(4) for h in range(2)] for y in range(4) for x in range(4) for c in range(2)]
BOTH = ("row", "col")
R4 = range(4)
Y_FLIP = {k: [(rid(z, y, c), rid(z, y ^ k, c)) for z in R4 for y in R4 for c in range(2)] for k in (1, 3)}
Z_FLIP = {k: [(rid(z, y, c), rid(z ^ k, y, c)) for z in R4 for y in R4 for c in range(2)] for k in (1, 3)}
X_FLIP = {k: [(q, q ^ k) for q in range(8)] for k in (1, 3)}
X_PERMS = [[(h * 4 + x, h * 4 + (x + k) % 4) for h in range(2) for x in R4] for k in (1, 2, 3)]
H_PERM = [(q, q ^ 4) for q in range(8)]


def in_hbm(*xs):
    return [pltpu.with_memory_space_constraint(x, pltpu.HBM) for x in xs]


def body(left, right, w_out, b_out, pair_grad):
    tie = lax.optimization_barrier
    g = pair_grad.reshape(IJ, Z)
    left_far = lax.ppermute(left, "col", H_PERM)
    (copies,) = copies_call(*in_hbm(right))
    right_own = lax.all_to_all(copies, "row", 0, 0, axis_index_groups=YZ)
    left_pair = jnp.stack([left, left_far])
    pieces = [left_pair] + [lax.ppermute(left_pair, "col", p) for p in X_PERMS]
    goh, gol, gr_own, gr_other, left_parts, g_parts, bias = grads_call(*pieces, *in_hbm(g, w_out))
    right_other = lax.ppermute(right_own, "row", CORE)
    oh, ol, bc, gw_own, gw_other = outer_call(left_parts, g_parts, bias, right_own, right_other)
    gw = gw_own + lax.ppermute(gw_other, "row", CORE)
    gw, goh, gol, bc = tie((gw, goh, gol, bc))
    gw = lax.all_to_all(gw, BOTH, 0, 0, axis_index_groups=XY)
    gr = gr_own + lax.ppermute(gr_other, "row", CORE)
    (gl,) = grad_left_call(*in_hbm(goh, gol, bc))
    (gw,) = spread_call(gw)
    gw, oh, ol = tie((gw, oh, ol))
    gr = gr[:2] + lax.ppermute(gr[2:], "row", Y_FLIP[1])
    gr = gr[0] + lax.ppermute(gr[1], "row", Y_FLIP[3])
    gl = gl[:2] + lax.ppermute(gl[2:], "col", X_FLIP[1])
    gl = gl[0] + lax.ppermute(gl[1], "col", X_FLIP[3])
    gw = lax.all_to_all(gw, BOTH, 0, 0, axis_index_groups=Z8)
    (pair_half,) = pair_calls[0](*in_hbm(oh, ol, w_out), b_out.reshape(1, Z))
    (pair_out,) = pair_calls[1](*in_hbm(oh, ol, w_out), b_out.reshape(1, Z), pair_half)
    gw, grad_bias = final_call(gw)
    gr = gr[:2] + lax.ppermute(gr[2:], "row", Z_FLIP[1])
    gr_part = lax.ppermute(gr[1], "row", Z_FLIP[3])
    gl_part = lax.ppermute(gl[1], "col", H_PERM)
    gw_own = lax.all_to_all(gw, BOTH, 0, 0, axis_index_groups=XY)
    gw_other = lax.ppermute(gw_own, "row", CORE)
    grad_weight, grad_right, grad_left = join_call(gw_own, gw_other, gr, gr_part, gl, gl_part)
    return (pair_out.reshape(TI, TJ, Z), grad_left, grad_right, grad_weight, grad_bias.reshape(Z))


def solution(mesh):
    placed = (P("col", "row"), P("row", "col"), P(), P(), P("row", "col", None))
    return jax.shard_map(
        body,
        mesh=mesh,
        in_specs=placed,
        out_specs=(P("row", "col", None), P("col", "row"), P("row", "col"), P(), P()),
        check_vma=False,
    )
```
